128 devices in a mesh: dp: 2 (over y_lo), ctx: 64 (over x, y_hi, z, core).
Axes of the slice: x: 4, y: 4 (y_hi: 2, y_lo: 2; y = y_hi * 2 + y_lo), z: 4, core: 2. Of those that a mesh axis runs over, the one named last changes fastest.
Arguments:
- tokens: bfloat16 [2, 24576, 2560], P('dp', 'ctx'), may hold values from -32 to 32
- qkv_weight: bfloat16 [2560, 3840], P(None, 'dp'), may hold values from -8 to 8
- out_weight: bfloat16 [1280, 2560], P(None, 'dp'), may hold values from -3.5 to 3.5
- offsets: int32 [4, 10], replicated, may hold values from 0 to 7, as said below
Outputs:
- mixed: bfloat16 [2, 24576, 2560], P('dp', 'ctx')
The draws below stay inside these ranges and needn't reach their ends.
Inputs may be any that keep to these rules, and one draw needn't show every extreme that they name: offsets[j, h] is at most 2 ** j - 1 for level j.
All inputs are finite; a program needn't handle non-finite values.
Results may differ from the reference program's by a relative error of at most 0.0083.
Values may be sent and summed in bfloat16 or wider, within the bound.
No kernel may reach another device: no remote copies, remote signals or barrier semaphores. Data moves between devices by JAX's collectives and lax.ppermute only.
A program may use at most 192 MiB of HBM per device.

```python
import jax
import jax.numpy as jnp
from jax import lax

D = 2560
HEADS = 10
HD = 128
LEVELS = 4
TOK_DEV = 384
BATCH = 2
SEQ = 24576


def draw_tokens(key, part):
    first_key = jax.random.fold_in(key, 0)
    drawn = jax.random.normal(first_key, (BATCH, SEQ, D), jnp.float32)
    return jnp.clip(drawn, -32.0, 32.0).astype(jnp.bfloat16)


def draw_qkv_weight(key, part):
    main_key = jax.random.fold_in(key, 0)
    drawn = jax.random.normal(main_key, (D, 3, HEADS, HD), jnp.float32) * D ** (-0.5)
    factors = jnp.array([1.2, 1.2, 1.0], jnp.float32)[None, :, None, None]
    drawn = drawn * factors
    return jnp.clip(drawn, -8.0, 8.0).reshape(D, 3 * HEADS * HD).astype(jnp.bfloat16)


def draw_offsets(key, part):
    limits = (2 ** jnp.arange(LEVELS, dtype=jnp.int32))[:, None]
    return jax.random.randint(key, (LEVELS, HEADS), 0, limits, dtype=jnp.int32)


def block_levels(key, extent, cuts, least, high):
    def one(axis_at, shards_of):
        steps = jax.random.uniform(jax.random.fold_in(jax.random.fold_in(key, 6), axis_at), (shards_of,), jnp.float32, least / len(cuts), high / len(cuts))
        return jnp.repeat(jnp.exp(steps), extent[axis_at] // shards_of).reshape((-1,) + (1,) * (len(extent) - axis_at - 1))

    level = one(*cuts[0])
    for cut in cuts[1:]:
        level = level * one(*cut)
    return level


def normal_values(own_key, extent, deviation, reach, cuts=(), kind=jnp.bfloat16):
    entries = deviation * jax.random.normal(own_key, extent, jnp.float32)
    if cuts:
        entries = entries * block_levels(own_key, extent, cuts, -0.22, 0.18)
    return jnp.clip(entries, -reach, reach).astype(kind)


def setup_inputs(seed: int = 0) -> dict:
    streams_of = jax.random.split(jax.random.key(seed), 5)
    tokens = draw_tokens(jax.random.fold_in(streams_of[4], 71), 0)
    qkv_weight = draw_qkv_weight(jax.random.fold_in(streams_of[4], 71), 0)
    out_weight = normal_values(streams_of[2], (HEADS * HD, D), (max(1, HEADS * HD // TOK_DEV)) ** -0.5, 3.5, ((1, 2),))
    offsets = draw_offsets(jax.random.fold_in(streams_of[4], 71), 0)
    return dict(tokens=tokens, qkv_weight=qkv_weight, out_weight=out_weight, offsets=offsets)


def attend(queries, key_rows, value_rows):
    scores = jnp.einsum("qhd,khd->hqk", queries.astype(jnp.float32), key_rows.astype(jnp.float32)) * (HD ** -0.5)
    row_max = jnp.max(scores, axis=2, keepdims=True)
    expo = jnp.exp(scores - row_max)
    row_total = jnp.sum(expo, axis=2)
    weights = expo.astype(jnp.bfloat16)
    blended = jnp.einsum("hqk,khd->qhd", weights.astype(jnp.float32), value_rows.astype(jnp.float32))
    blended = blended / row_total.T[:, :, None]
    return blended, (row_max[:, :, 0] + jnp.log(row_total)).T


def attend_triple(triple):
    return attend(triple[0], triple[1], triple[2])


def choose(values_in, chosen, dilation):
    array_shape = values_in.shape
    grouped = values_in.reshape(array_shape[0], array_shape[1] // dilation, dilation, array_shape[2], array_shape[3])
    return jnp.sum(jnp.where(chosen[None, None, :, :, None], grouped, jnp.zeros((), grouped.dtype)), axis=2)


def reference(tokens, qkv_weight, out_weight, offsets):
    projected = jnp.dot(tokens.reshape(BATCH * SEQ, D), qkv_weight, preferred_element_type=jnp.float32)
    projected = projected.astype(jnp.bfloat16).reshape(BATCH, SEQ, 3, HEADS, HD)
    all_query = projected[:, :, 0]
    all_key = projected[:, :, 1]
    all_value = projected[:, :, 2]
    span = 2 * TOK_DEV
    for degree in range(LEVELS):
        dilation = 2 ** degree
        chosen = jnp.arange(dilation, dtype=jnp.int32)[:, None] == offsets[degree][None, :]
        picked_query = choose(all_query, chosen, dilation).reshape(-1, span, HEADS, HD)
        picked_key = choose(all_key, chosen, dilation).reshape(-1, span, HEADS, HD)
        picked_value = choose(all_value, chosen, dilation).reshape(-1, span, HEADS, HD)
        blended, row_lse = lax.map(attend_triple, (picked_query, picked_key, picked_value))
        blended = blended.reshape(BATCH, SEQ // dilation, HEADS, HD)
        row_lse = row_lse.reshape(BATCH, SEQ // dilation, HEADS)
        level_out = jnp.where(chosen[None, None, :, :, None], blended[:, :, None], 0.0).reshape(BATCH, SEQ, HEADS, HD)
        level_lse = jnp.where(chosen[None, None], row_lse[:, :, None], -jnp.inf).reshape(BATCH, SEQ, HEADS)
        if degree == 0:
            weighted = level_out
            totals = jnp.ones_like(level_lse)
            running = level_lse
        else:
            newest = jnp.maximum(running, level_lse)
            former = jnp.exp(running - newest)
            fresh = jnp.exp(level_lse - newest)
            weighted = weighted * former[..., None] + fresh[..., None] * level_out
            totals = totals * former + fresh
            running = newest
    attended = (weighted / totals[..., None]).astype(jnp.bfloat16).reshape(BATCH * SEQ, HEADS * HD)
    mixed = jnp.dot(attended, out_weight, preferred_element_type=jnp.float32).astype(jnp.bfloat16)
    return mixed.reshape(BATCH, SEQ, D)
```

```python
import jax
import jax.numpy as jnp
from jax import lax
from jax.experimental import pallas as pl
from jax.experimental.pallas import tpu as pltpu
from jax.sharding import PartitionSpec as P


TOK = 384
ROWS = 2 * TOK
HD = 128
HH = 5
WB = HH * HD
LEVELS = 4
KC = 640
LOG2E = 1.4426950408889634

META_CORE, META_FSRC, META_FBLK, META_SSRC, META_SBLK, META_QSRC, META_QBLK, META_FK, META_DP = range(9)
META_OFF = 16


def lin(x, y, z, c):
    return (y % 2) * 64 + (((x % 4) * 2 + (y % 4) // 2) * 4 + z % 4) * 2 + c


def send(block, target):
    route = []
    for x in range(4):
        for y in range(4):
            for z in range(4):
                for c in range(2):
                    goal = target(x, y, z, c)
                    if goal is not None:
                        route.append((lin(x, y, z, c), lin(*goal)))
    return lax.ppermute(block, ("dp", "ctx"), route)


def to_core(x, y, z, c):
    return (x, y, z, 1 - c)


def to_y(x, y, z, c):
    return (x, y - 1 if c == 0 else y + 1, z, c)


def to_x(x, y, z, c):
    return (x, y, z, c) if False else (x - 1 if c == 0 else x + 1, y, z, c)


def to_z1(x, y, z, c):
    return (x, y, z ^ 1, c)


def to_z3(x, y, z, c):
    return (x, y, z ^ 3, c)


def to_y2(x, y, z, c):
    return (x, y + 2, z, c)


def to_main(x, y, z, c):
    main = 1 if y % 2 == 0 else 0
    return (x, y, z, main) if c != main else None


def to_side(x, y, z, c):
    main = 1 if y % 2 == 0 else 0
    return (x, y, z, 1 - main) if c == main else None


def proj_kernel(remote, slot, meta, x_own, x_oth, w_loc, *rest):
    halves = rest[: 2 * remote]
    outs = rest[2 * remote : 2 * remote + LEVELS]
    xbuf, wbuf, acc, xsem, wsem = rest[2 * remote + LEVELS :]
    chunks = w_loc.shape[0] // KC
    core = meta[META_CORE]
    src = meta[slot]
    col = pl.multiple_of(meta[slot + 1] * WB, HD)
    for i in range(chunks):
        rows = pl.ds(i * KC, KC)
        pltpu.make_async_copy(x_own.at[:, rows], xbuf.at[pl.ds(0, TOK), rows], xsem.at[i, 0]).start()
        pltpu.make_async_copy(x_oth.at[:, rows], xbuf.at[pl.ds(TOK, TOK), rows], xsem.at[i, 1]).start()

        @pl.when(src == 0)
        def _():
            pltpu.make_async_copy(w_loc.at[rows, pl.ds(col, WB)], wbuf.at[rows], wsem.at[i]).start()

        part = i * 2 // chunks
        low = pl.ds((i - part * (chunks // 2)) * KC, KC)
        for r in range(remote):
            for own in range(2):

                @pl.when((src == r + 1) & ((core == part) if own else (core != part)))
                def _():
                    pltpu.make_async_copy(halves[2 * r + 1 - own].at[low], wbuf.at[rows], wsem.at[i]).start()

    for i in range(chunks):
        rows = pl.ds(i * KC, KC)
        pltpu.make_async_copy(x_own.at[:, rows], xbuf.at[pl.ds(0, TOK), rows], xsem.at[i, 0]).wait()
        pltpu.make_async_copy(x_oth.at[:, rows], xbuf.at[pl.ds(TOK, TOK), rows], xsem.at[i, 1]).wait()
        pltpu.make_async_copy(w_loc.at[rows, pl.ds(0, WB)], wbuf.at[rows], wsem.at[i]).wait()
        for g in range(2):
            span = pl.ds(g * TOK, TOK)
            got = jnp.dot(xbuf[span, rows], wbuf[rows], preferred_element_type=jnp.float32)
            for h in range(HH):
                piece = got[:, h * HD : (h + 1) * HD]
                if i > 0:
                    piece = acc[h, span] + piece
                if i < chunks - 1:
                    acc[h, span] = piece
                else:
                    acc[h, span] = piece
                    outs[0][span, pl.ds(h * HD, HD)] = piece.astype(jnp.bfloat16)
    for h in range(HH):
        for j in range(1, LEVELS):
            off = meta[META_OFF + j * HH + h]
            kept = acc[h, pl.ds(off, ROWS >> j, stride=1 << j), :]
            outs[j][:, pl.ds(h * HD, HD)] = kept.astype(jnp.bfloat16)


def project(meta, slot, x_own, x_oth, w_loc, remotes):
    depth = w_loc.shape[0]
    anywhere = pl.BlockSpec(memory_space=pl.ANY)
    flat = [half for pair in remotes for half in pair]
    return pl.pallas_call(
        lambda *refs: proj_kernel(len(remotes), slot, *refs),
        out_shape=[jax.ShapeDtypeStruct((ROWS >> j, WB), jnp.bfloat16) for j in range(LEVELS)],
        in_specs=[pl.BlockSpec(memory_space=pltpu.SMEM)] + [anywhere] * (3 + len(flat)),
        out_specs=[pl.BlockSpec(memory_space=pltpu.VMEM)] * LEVELS,
        scratch_shapes=[
            pltpu.VMEM((ROWS, depth), jnp.bfloat16),
            pltpu.VMEM((depth, WB), jnp.bfloat16),
            pltpu.VMEM((HH, ROWS, HD), jnp.float32),
            pltpu.SemaphoreType.DMA((depth // KC, 2)),
            pltpu.SemaphoreType.DMA((depth // KC,)),
        ],
        name=f"project{slot}",
        cost_estimate=pl.CostEstimate(
            flops=2 * ROWS * depth * WB, transcendentals=0, bytes_accessed=2 * (ROWS * depth + depth * WB + 2 * ROWS * WB)
        ),
    )(meta, x_own, x_oth, w_loc, *flat)


def attn_kernel(level, counts, last, scale, meta, *refs):
    pieces = len(counts)
    q_ref = refs[0]
    firsts, seconds = refs[1 : 1 + pieces], refs[1 + pieces : 1 + 2 * pieces]
    rest = refs[1 + 2 * pieces :]
    head = pl.program_id(0)
    f_is_k = jnp.full((1, 1), meta[META_FK], jnp.int32) == 1
    keys, values = [], []
    for f_ref, s_ref in zip(firsts, seconds):
        f = f_ref[...].reshape(-1, HD)
        s = s_ref[...].reshape(-1, HD)
        keys.append(jnp.where(f_is_k, f, s))
        values.append(jnp.where(f_is_k, s, f))
    rows = q_ref.shape[0]
    step = min(rows, 192)
    if level == 0:
        acc_ref, ml_ref = rest
    elif last:
        acc_in, ml_in, out_ref, acc_ref, ml_ref = rest
        acc_ref[...] = acc_in[...]
        ml_ref[...] = ml_in[0]
    else:
        acc_in, ml_in, acc_ref, ml_ref, acc_s, ml_s = rest
        acc_s[...] = acc_in[...]
        ml_s[...] = ml_in[0]
    off = meta[META_OFF + level * HH + head]
    lane = lax.broadcasted_iota(jnp.int32, (1, HD), 1)
    for start in range(0, rows, step):
        q = q_ref[pl.ds(start, step), :]
        scores = [
            lax.dot_general(q, k, (((1,), (1,)), ((), ())), preferred_element_type=jnp.float32) for k in keys
        ]
        top = scores[0].max(axis=1, keepdims=True)
        for s in scores[1:]:
            top = jnp.maximum(top, s.max(axis=1, keepdims=True))
        total = jnp.zeros((step, 1), jnp.float32)
        blend = jnp.zeros((step, HD), jnp.float32)
        for s, v in zip(scores, values):
            e = jnp.exp2((s - top) * (scale * LOG2E))
            total = total + e.sum(axis=1, keepdims=True)
            blend = blend + jnp.dot(e.astype(jnp.bfloat16), v, preferred_element_type=jnp.float32)
        top = top * (scale * LOG2E)
        if level == 0:
            acc_ref[pl.ds(start, step), :] = blend
            ml_ref[0, pl.ds(start, step), :] = jnp.where(lane == 0, top, total)
        else:
            a_ref, m_ref = (acc_ref, ml_ref) if last else (acc_s, ml_s)
            where = pl.ds(off + (start << level), step, stride=1 << level)
            old = m_ref[where, :]
            old_top, old_total = old[:, 0:1], old[:, 1:2]
            newest = jnp.maximum(old_top, top)
            former, fresh = jnp.exp2(old_top - newest), jnp.exp2(top - newest)
            a_ref[where, :] = a_ref[where, :] * former + blend * fresh
            m_ref[where, :] = jnp.where(lane == 0, newest, old_total * former + total * fresh)
    if last:
        out_ref[...] = (acc_ref[...] / ml_ref[:, 1:2]).astype(jnp.bfloat16)
    elif level > 0:
        acc_ref[...] = acc_s[...]
        ml_ref[0] = ml_s[...]


def attend(meta, level, q, firsts, seconds, state, scale, last=False):
    rows = q.shape[0]
    counts = [f.size // WB for f in firsts]

    def lanes(a):
        lead = a.shape[:-1]
        return pl.BlockSpec(lead + (HD,), lambda h: (0,) * len(lead) + (h,))

    acc_spec = pl.BlockSpec((ROWS, HD), lambda h: (0, h))
    ml_spec = pl.BlockSpec((1, ROWS, HD), lambda h: (h, 0, 0))
    acc_shape = jax.ShapeDtypeStruct((ROWS, WB), jnp.float32)
    ml_shape = jax.ShapeDtypeStruct((HH, ROWS, HD), jnp.float32)
    ins = [meta, q, *firsts, *seconds]
    specs = [pl.BlockSpec(memory_space=pltpu.SMEM)] + [lanes(a) for a in ins[1:]]
    if level > 0:
        ins += list(state)
        specs += [acc_spec, ml_spec]
    scratch = [] if level == 0 else [pltpu.VMEM((ROWS, HD), jnp.float32), pltpu.VMEM((ROWS, HD), jnp.float32)]
    if last:
        out_shape, out_specs = jax.ShapeDtypeStruct((ROWS, WB), jnp.bfloat16), acc_spec
    else:
        out_shape, out_specs = [acc_shape, ml_shape], [acc_spec, ml_spec]
    keys = sum(counts)
    return pl.pallas_call(
        lambda *refs: attn_kernel(level, counts, last, scale, *refs),
        grid=(HH,),
        in_specs=specs,
        out_specs=out_specs,
        out_shape=out_shape,
        scratch_shapes=scratch,
        name=f"attend{level}",
        cost_estimate=pl.CostEstimate(
            flops=4 * rows * keys * WB, transcendentals=rows * keys * HH, bytes_accessed=2 * (rows + 2 * keys) * WB + 16 * ROWS * WB
        ),
    )(*ins)


def out_kernel(meta, own, oth, loc_a, loc_b, rem_a, rem_b, out):
    t = pl.program_id(0)

    def run(a, b):
        got = jnp.dot(own[...], a[...], preferred_element_type=jnp.float32)
        got = got + jnp.dot(oth[...], b[...], preferred_element_type=jnp.float32)
        out[...] = got.astype(jnp.bfloat16)

    @pl.when(t < 2)
    def _():
        run(loc_a, loc_b)

    @pl.when(t >= 2)
    def _():
        run(rem_a, rem_b)


def out_project(meta, att, oth, w_loc, rem_own, rem_oth):
    wide = w_loc.shape[1]
    tile = wide // 2
    grid_spec = pltpu.PrefetchScalarGridSpec(
        num_scalar_prefetch=1,
        grid=(4,),
        in_specs=[
            pl.BlockSpec((TOK, WB), lambda t, m: (0, 0)),
            pl.BlockSpec((TOK, WB), lambda t, m: (0, 0)),
            pl.BlockSpec((WB, tile), lambda t, m: (m[META_CORE], jnp.minimum(t, 1))),
            pl.BlockSpec((WB, tile), lambda t, m: (1 - m[META_CORE], jnp.minimum(t, 1))),
            pl.BlockSpec((WB, tile), lambda t, m: (0, jnp.maximum(t - 2, 0))),
            pl.BlockSpec((WB, tile), lambda t, m: (0, jnp.maximum(t - 2, 0))),
        ],
        out_specs=pl.BlockSpec(
            (TOK, tile), lambda t, m: (0, jnp.where(t < 2, m[META_DP] * 2 + t, (1 - m[META_DP]) * 2 + t - 2))
        ),
    )
    return pl.pallas_call(
        out_kernel,
        grid_spec=grid_spec,
        out_shape=jax.ShapeDtypeStruct((TOK, 2 * wide), jnp.bfloat16),
        name="outproj",
        cost_estimate=pl.CostEstimate(
            flops=2 * TOK * 2 * WB * 2 * wide, transcendentals=0, bytes_accessed=2 * (TOK * 2 * WB + 4 * WB * wide + 2 * TOK * wide)
        ),
    )(meta, att, oth, w_loc, w_loc, rem_own, rem_oth)


def local(tokens, qkv_weight, out_weight, offsets):
    d = lax.axis_index("dp")
    ctx = lax.axis_index("ctx")
    core = ctx & 1
    odd = (ctx >> 4) & 1
    main = 1 - d
    is_main = core == main
    depth = qkv_weight.shape[0]
    half = depth // 2
    scale = HD ** (-0.5)

    pick = lambda a0, a1, b0, b1: jnp.where(d == 0, jnp.where(core == 0, a0, a1), jnp.where(core == 0, b0, b1))
    f_src, f_blk = pick(0, 1, 0, 0), pick(2, 0, 1, 0)
    s_src, s_blk = pick(3, 2, 1 + odd, 0), pick(0, 0, 0, 2)
    q_src, q_blk = pick(0, 0, 2 - odd, 3), pick(0, 1, 0, 0)
    f_is_k = pick(1, 1 - odd, 0, 1)
    zero = jnp.zeros((), jnp.int32)
    heads = lax.dynamic_slice(offsets, (0, core * HH), (LEVELS, HH)).reshape(-1)
    meta = jnp.concatenate(
        [jnp.stack([core, f_src, f_blk, s_src, s_blk, q_src, q_blk, f_is_k, d] + [zero] * 7).astype(jnp.int32), heads]
    )

    first_blk = jnp.where((d ^ odd) == 0, 2, 0)
    pay_first = lax.dynamic_slice(qkv_weight, (core * half, first_blk * WB), (half, WB))
    pay_side = lax.dynamic_slice(qkv_weight, (core * half, zero + WB), (half, WB))
    x_own = tokens.reshape(TOK, depth)
    first_own = send(pay_first, to_y)
    side_own = send(pay_side, to_y)
    x_oth = send(x_own, to_core)
    first_fwd = send(first_own, to_main)
    relay_own = send(first_own, to_x)
    relay_fwd = send(relay_own, to_main)
    side_fwd = send(side_own, to_side)

    first = project(meta, META_FSRC, x_own, x_oth, qkv_weight, [(first_own, first_fwd)])

    def gather(blocks):
        _, b1, b2, b3 = blocks
        b2_pair = send(b2, to_z1)
        b3_far = send(b3, to_y2)
        b2_ring = send(b2, to_z3)
        b3_both = jnp.stack([b3, b3_far])
        b3_pair = send(b3_both, to_z1)
        b2_relay = send(b2_pair, to_z3)
        b3_ring = send(b3_both, to_z3)
        b1_pair = send(b1, to_z1)
        b3_relay = send(b3_pair, to_z3)
        return [[blocks[0]], [b1, b1_pair], [b2, b2_pair, b2_ring, b2_relay], [b3_both, b3_pair, b3_ring, b3_relay]]

    f_pieces = gather(first)
    everything = [(first_own, first_fwd), (relay_own, relay_fwd), (side_own, side_fwd)]
    second = project(meta, META_SSRC, x_own, x_oth, qkv_weight, everything)
    s_pieces = gather(second)
    queries = project(meta, META_QSRC, x_own, x_oth, qkv_weight, everything)

    w_own = lax.dynamic_slice(out_weight, (core * WB, zero), (WB, out_weight.shape[1]))
    rem_own = send(w_own, to_y)
    rem_oth = send(rem_own, to_core)

    state = attend(meta, 0, queries[0], f_pieces[0], s_pieces[0], None, scale)
    state = attend(meta, 2, queries[2], f_pieces[2], s_pieces[2], state, scale)
    state = attend(meta, 1, queries[1], f_pieces[1], s_pieces[1], state, scale)
    att = attend(meta, 3, queries[3], f_pieces[3], s_pieces[3], state, scale, last=True)
    att_oth = send(att[TOK:], to_core)
    mixed = out_project(meta, att, att_oth, out_weight, rem_own, rem_oth)
    return mixed.reshape(1, TOK, mixed.shape[1])


def solution(mesh):
    in_specs = (P("dp", "ctx", None), P(None, "dp"), P(None, "dp"), P())
    out_specs = P("dp", "ctx", None)
    return jax.shard_map(local, mesh=mesh, in_specs=in_specs, out_specs=out_specs, check_vma=False)
```

```python
import jax
import jax.numpy as jnp
from jax import lax
from jax.experimental import pallas as pl
from jax.experimental.pallas import tpu as pltpu
from jax.sharding import PartitionSpec as P


TOK = 384
ROWS = 2 * TOK
HD = 128
HH = 5
WB = HH * HD
LEVELS = 4
KC = 1280
LOG2E = 1.4426950408889634

META_CORE, META_FSRC, META_FBLK, META_SSRC, META_SBLK, META_QSRC, META_QBLK, META_FK, META_DP = range(9)
META_OFF = 16


def lin(x, y, z, c):
    return (y % 2) * 64 + (((x % 4) * 2 + (y % 4) // 2) * 4 + z % 4) * 2 + c


def send(block, target):
    route = []
    for x in range(4):
        for y in range(4):
            for z in range(4):
                for c in range(2):
                    goal = target(x, y, z, c)
                    if goal is not None:
                        route.append((lin(x, y, z, c), lin(*goal)))
    return lax.ppermute(block, ("dp", "ctx"), route)


def to_core(x, y, z, c):
    return (x, y, z, 1 - c)


def to_y(x, y, z, c):
    return (x, y - 1 if c == 0 else y + 1, z, c)


def to_x(x, y, z, c):
    return (x - 1 if c == 0 else x + 1, y, z, c)


def to_z1(x, y, z, c):
    return (x, y, z ^ 1, c)


def to_z3(x, y, z, c):
    return (x, y, z ^ 3, c)


def to_y2(x, y, z, c):
    return (x, y + 2, z, c)


def to_main(x, y, z, c):
    main = 1 if y % 2 == 0 else 0
    return (x, y, z, main) if c != main else None


def to_side(x, y, z, c):
    main = 1 if y % 2 == 0 else 0
    return (x, y, z, 1 - main) if c == main else None


def held(*arrays):
    return [pltpu.with_memory_space_constraint(a, pltpu.VMEM) for a in arrays]


HELD = pl.BlockSpec(memory_space=pltpu.VMEM)
SCALARS = pl.BlockSpec(memory_space=pltpu.SMEM)
ANYWHERE = pl.BlockSpec(memory_space=pl.ANY)


def params(mib):
    return pltpu.CompilerParams(vmem_limit_bytes=mib << 20)


CUT2, CUT3 = ROWS >> 2, (ROWS >> 2) + (ROWS >> 3)


def proj_kernel(remote, slot, for_keys, meta, x_own, x_oth, w_loc, *rest):
    halves = rest[: 2 * remote]
    outs, (wbuf, acc, wsem) = rest[2 * remote : -3], rest[-3:]
    chunks = w_loc.shape[0] // KC
    core = meta[META_CORE]
    src = meta[slot]
    col = pl.multiple_of(meta[slot + 1] * WB, HD)
    for i in range(chunks):
        rows = pl.ds(i * KC, KC)

        @pl.when(src == 0)
        def _():
            pltpu.make_async_copy(w_loc.at[rows, pl.ds(col, WB)], wbuf.at[rows], wsem.at[i]).start()

        part = i * 2 // chunks
        low = pl.ds((i - part * (chunks // 2)) * KC, KC)
        for r in range(remote):
            for own in range(2):

                @pl.when((src == r + 1) & ((core == part) if own else (core != part)))
                def _():
                    pltpu.make_async_copy(halves[2 * r + 1 - own].at[low], wbuf.at[rows], wsem.at[i]).start()

    for i in range(chunks):
        rows = pl.ds(i * KC, KC)
        pltpu.make_async_copy(w_loc.at[rows, pl.ds(0, WB)], wbuf.at[rows], wsem.at[i]).wait()
        for g, x_ref in enumerate((x_own, x_oth)):
            span = pl.ds(g * TOK, TOK)
            got = jnp.dot(x_ref[:, rows], wbuf[rows], preferred_element_type=jnp.float32)
            for h in range(HH):
                piece = got[:, h * HD : (h + 1) * HD]
                if i > 0:
                    piece = acc[h, span] + piece
                acc[h, span] = piece
                if i == chunks - 1:
                    outs[0][span, pl.ds(h * HD, HD)] = piece.astype(jnp.bfloat16)
    for h in range(HH):
        cols = pl.ds(h * HD, HD)
        kept = [
            acc[h, pl.ds(meta[META_OFF + j * HH + h], ROWS >> j, stride=1 << j), :].astype(jnp.bfloat16)
            for j in range(1, LEVELS)
        ]
        outs[1][:, cols] = kept[0]
        outs[2][pl.ds(0, CUT2), cols] = kept[1]
        outs[2][pl.ds(CUT2, ROWS >> 3), cols] = kept[2]
        if for_keys:
            outs[2][pl.ds(CUT3, ROWS >> 3), cols] = kept[2]
            outs[3][:, cols] = kept[2]


def project(meta, slot, x_own, x_oth, w_loc, remotes, for_keys):
    depth = w_loc.shape[0]
    flat = [half for pair in remotes for half in pair]
    shapes = [(ROWS, WB), (ROWS >> 1, WB)] + ([(ROWS >> 1, WB), (ROWS >> 3, WB)] if for_keys else [(CUT3, WB)])
    return pl.pallas_call(
        lambda *refs: proj_kernel(len(remotes), slot, for_keys, *refs),
        out_shape=[pltpu.VMEM(s, jnp.bfloat16) for s in shapes],
        in_specs=[SCALARS, HELD, HELD] + [ANYWHERE] * (1 + len(flat)),
        out_specs=[HELD] * len(shapes),
        scratch_shapes=[
            pltpu.VMEM((depth, WB), jnp.bfloat16),
            pltpu.VMEM((HH, ROWS, HD), jnp.float32),
            pltpu.SemaphoreType.DMA((depth // KC,)),
        ],
        compiler_params=params(16),
        name=f"project{slot}",
        cost_estimate=pl.CostEstimate(
            flops=2 * ROWS * depth * WB, transcendentals=0, bytes_accessed=2 * (ROWS * depth + depth * WB + 2 * ROWS * WB)
        ),
    )(meta, *held(x_own, x_oth), w_loc, *flat)


def softmax_rows(q, keys, values, factor):
    scores = [lax.dot_general(q, k, (((1,), (1,)), ((), ())), preferred_element_type=jnp.float32) for k in keys]
    top = scores[0].max(axis=1, keepdims=True)
    for s in scores[1:]:
        top = jnp.maximum(top, s.max(axis=1, keepdims=True))
    total, blend = 0.0, 0.0
    for s, v in zip(scores, values):
        e = jnp.exp2((s - top) * factor)
        total = total + e.sum(axis=1, keepdims=True)
        blend = blend + jnp.dot(e.astype(jnp.bfloat16), v, preferred_element_type=jnp.float32)
    return blend, top * factor, total


def pack(top, total):
    lane = lax.broadcasted_iota(jnp.int32, (1, HD), 1)
    return jnp.where(lane == 0, top, total)


def merge(acc_ref, ml_ref, where, blend, top, total):
    old = ml_ref[where]
    old_top, old_total = old[:, 0:1], old[:, 1:2]
    newest = jnp.maximum(old_top, top)
    former, fresh = jnp.exp2(old_top - newest), jnp.exp2(top - newest)
    acc_ref[where] = acc_ref[where] * former + blend * fresh
    ml_ref[where] = pack(newest, old_total * former + total * fresh)


def choose(meta, firsts, seconds, cut, cols):
    f_is_k = jnp.full((1, 1), meta[META_FK], jnp.int32) == 1
    keys, values = [], []
    for f_ref, s_ref in zip(firsts, seconds):
        f, s = f_ref[cut, cols], s_ref[cut, cols]
        keys.append(jnp.where(f_is_k, f, s))
        values.append(jnp.where(f_is_k, s, f))
    return keys, values


def level0_kernel(factor, meta, q_ref, f_ref, s_ref, acc_ref, ml_ref):
    for h in range(HH):
        cols = pl.ds(h * HD, HD)
        keys, values = choose(meta, [f_ref], [s_ref], slice(None), cols)
        for start in range(0, ROWS, TOK):
            blend, top, total = softmax_rows(q_ref[pl.ds(start, TOK), cols], keys, values, factor)
            acc_ref[h, pl.ds(start, TOK), :] = blend
            ml_ref[h, pl.ds(start, TOK), :] = pack(top, total)


def level1_kernel(factor, meta, q_ref, f0, f1, s0, s1, acc_in, ml_in, acc_ref, ml_ref):
    for h in range(HH):
        cols = pl.ds(h * HD, HD)
        keys, values = choose(meta, [f0, f1], [s0, s1], slice(None), cols)
        acc_ref[h] = acc_in[h]
        ml_ref[h] = ml_in[h]
        where = (h, pl.ds(meta[META_OFF + HH + h], TOK, stride=2), slice(None))
        merge(acc_ref, ml_ref, where, *softmax_rows(q_ref[:, cols], keys, values, factor))


def level23_kernel(factor, meta, q_ref, f0, f1, f2, f3, s0, s1, s2, s3, acc_in, ml_in, own_ref, oth_ref, acc, ml):
    for h in range(HH):
        cols = pl.ds(h * HD, HD)
        acc[h] = acc_in[h]
        ml[h] = ml_in[h]
        for level, low, rows in ((2, 0, CUT2), (3, CUT2, ROWS >> 3)):
            cut = slice(0, CUT2) if level == 2 else slice(CUT2, ROWS >> 1)
            keys, values = choose(meta, [f0, f1, f2, f3], [s0, s1, s2, s3], cut, cols)
            where = (h, pl.ds(meta[META_OFF + level * HH + h], rows, stride=1 << level), slice(None))
            merge(acc, ml, where, *softmax_rows(q_ref[pl.ds(low, rows), cols], keys, values, factor))
        share = acc[h] * (1.0 / ml[h][:, 1:2])
        own_ref[:, cols] = share[:TOK].astype(jnp.bfloat16)
        oth_ref[:, cols] = share[TOK:].astype(jnp.bfloat16)


STATE = [((HH, ROWS, HD), jnp.float32)] * 2


def attend(kernel, name, meta, arrays, outs, rows, scratch=()):
    factor = HD ** (-0.5) * LOG2E
    return pl.pallas_call(
        lambda *refs: kernel(factor, *refs),
        out_shape=[pltpu.VMEM(*o) for o in outs],
        in_specs=[SCALARS] + [HELD] * len(arrays),
        out_specs=[HELD] * len(outs),
        scratch_shapes=[pltpu.VMEM(*s) for s in scratch],
        compiler_params=params(20),
        name=name,
        cost_estimate=pl.CostEstimate(
            flops=4 * rows * ROWS * WB, transcendentals=rows * ROWS * HH, bytes_accessed=2 * (rows + 2 * ROWS) * WB
        ),
    )(meta, *held(*arrays))


def tile_of(t, core_rows, w_loc, rem):
    cols = pl.ds((t % 2) * WB, WB)
    return w_loc[core_rows, cols] if t < 2 else rem[:, cols]


def out_own_kernel(meta, att, w_loc, rem, part):
    rows = pl.ds(pl.multiple_of(meta[META_CORE] * WB, HD), WB)
    for t in range(4):
        part[t] = jnp.dot(att[...], tile_of(t, rows, w_loc, rem), preferred_element_type=jnp.float32)


def out_oth_kernel(meta, att, w_loc, rem, part, out, buf, sem):
    rows = pl.ds(pl.multiple_of((1 - meta[META_CORE]) * WB, HD), WB)
    d = meta[META_DP]
    copies = []
    for t in range(4):
        got = part[t] + jnp.dot(att[...], tile_of(t, rows, w_loc, rem), preferred_element_type=jnp.float32)
        buf[t] = got.astype(jnp.bfloat16)
        col = (d if t < 2 else 1 - d) * (2 * WB) + (t % 2) * WB
        copies.append(pltpu.make_async_copy(buf.at[t], out.at[:, pl.ds(pl.multiple_of(col, HD), WB)], sem.at[t]))
        copies[-1].start()
    for copy in copies:
        copy.wait()


def out_project(kernel, name, meta, arrays, out_shape, out_spec, scratch):
    return pl.pallas_call(
        kernel,
        out_shape=out_shape,
        in_specs=[SCALARS] + [HELD] * len(arrays),
        out_specs=out_spec,
        scratch_shapes=scratch,
        compiler_params=params(16),
        name=name,
        cost_estimate=pl.CostEstimate(flops=8 * TOK * WB * WB, transcendentals=0, bytes_accessed=8 * WB * WB + 8 * TOK * WB),
    )(meta, *held(*arrays))


def after(value, *others):
    return lax.optimization_barrier((value, *others))[0]


def local(tokens, qkv_weight, out_weight, offsets):
    d = lax.axis_index("dp")
    ctx = lax.axis_index("ctx")
    core = ctx & 1
    odd = (ctx >> 4) & 1
    depth = qkv_weight.shape[0]
    half = depth // 2

    pick = lambda a0, a1, b0, b1: jnp.where(d == 0, jnp.where(core == 0, a0, a1), jnp.where(core == 0, b0, b1))
    f_src, f_blk = pick(0, 1, 0, 0), pick(2, 0, 1, 0)
    s_src, s_blk = pick(3, 2, 1 + odd, 0), pick(0, 0, 0, 2)
    q_src, q_blk = pick(0, 0, 2 - odd, 3), pick(0, 1, 0, 0)
    f_is_k = pick(1, 1 - odd, 0, 1)
    zero = jnp.zeros((), jnp.int32)
    heads = lax.dynamic_slice(offsets, (0, core * HH), (LEVELS, HH)).reshape(-1)
    meta = jnp.concatenate(
        [jnp.stack([core, f_src, f_blk, s_src, s_blk, q_src, q_blk, f_is_k, d] + [zero] * 7).astype(jnp.int32), heads]
    )

    first_blk = jnp.where((d ^ odd) == 0, 2, 0)
    pay_first = lax.dynamic_slice(qkv_weight, (core * half, first_blk * WB), (half, WB))
    x_own = tokens.reshape(TOK, depth)
    x_oth = send(x_own, to_core)
    first_own = send(pay_first, to_y)
    pay_side = lax.dynamic_slice(after(qkv_weight, pay_first), (core * half, zero + WB), (half, WB))
    side_own = send(pay_side, to_y)
    first_fwd = send(first_own, to_main)
    relay_own = send(first_own, to_x)

    first = project(meta, META_FSRC, x_own, x_oth, qkv_weight, [(first_own, first_fwd)], True)
    side_own = after(side_own, first[3])
    relay_own = after(relay_own, first[3])
    relay_fwd = send(relay_own, to_main)
    side_fwd = send(side_own, to_side)

    def gather(b23, far):
        joined = lax.dynamic_update_slice(b23, far, (CUT3, 0))
        pair = send(joined, to_z1)
        ring = send(joined, to_z3)
        return joined, pair, ring, send(pair, to_z3)

    f1_pair, f_far = None, send(first[3], to_y2)
    f23 = gather(first[2], f_far)
    f1_pair = send(first[1], to_z1)
    everything = [(first_own, first_fwd), (relay_own, relay_fwd), (side_own, side_fwd)]
    second = project(meta, META_SSRC, x_own, x_oth, qkv_weight, everything, True)
    s_far = send(second[3], to_y2)
    queries = project(meta, META_QSRC, after(x_own, second[3]), x_oth, qkv_weight, everything, False)
    s23 = gather(second[2], s_far)
    s1_pair = send(second[1], to_z1)

    w_own = lax.dynamic_slice(after(out_weight, second[3]), (core * WB, zero), (WB, out_weight.shape[1]))
    rem_own = send(w_own, to_y)
    rem_oth = send(rem_own, to_core)

    state = attend(level0_kernel, "level0", meta, [queries[0], first[0], second[0]], STATE, ROWS)
    state = attend(level1_kernel, "level1", meta, [queries[1], first[1], f1_pair, second[1], s1_pair, *state], STATE, ROWS >> 1)
    att, att_send = attend(
        level23_kernel, "level23", meta, [queries[2], *f23, *s23, *state], [((TOK, WB), jnp.bfloat16)] * 2, CUT3, STATE
    )
    att_oth = send(att_send, to_core)
    part = out_project(
        out_own_kernel, "outown", meta, [att, out_weight, rem_own], pltpu.VMEM((4, TOK, WB), jnp.float32), HELD, []
    )
    mixed = out_project(
        out_oth_kernel,
        "outoth",
        meta,
        [att_oth, out_weight, rem_oth, part],
        jax.ShapeDtypeStruct((TOK, 4 * WB), jnp.bfloat16),
        ANYWHERE,
        [pltpu.VMEM((4, TOK, WB), jnp.bfloat16), pltpu.SemaphoreType.DMA((4,))],
    )
    return mixed.reshape(1, TOK, mixed.shape[1])


def solution(mesh):
    in_specs = (P("dp", "ctx", None), P(None, "dp"), P(None, "dp"), P())
    out_specs = P("dp", "ctx", None)
    return jax.shard_map(local, mesh=mesh, in_specs=in_specs, out_specs=out_specs, check_vma=False)
```

```python
import jax
import jax.numpy as jnp
from jax import lax
from jax.experimental import pallas as pl
from jax.experimental.pallas import tpu as pltpu
from jax.sharding import PartitionSpec as P


TOK = 384
ROWS = 2 * TOK
HD = 128
HH = 5
WB = HH * HD
LEVELS = 4
KC = 1280
LOG2E = 1.4426950408889634

META_CORE, META_FSRC, _, META_SSRC, _, META_QSRC, _, META_FK, META_DP = range(9)
META_OFF = 16


def lin(x, y, z, c):
    return (y % 2) * 64 + (((x % 4) * 2 + (y % 4) // 2) * 4 + z % 4) * 2 + c


def send(block, target):
    route = []
    for x in range(4):
        for y in range(4):
            for z in range(4):
                for c in range(2):
                    goal = target(x, y, z, c)
                    if goal is not None:
                        route.append((lin(x, y, z, c), lin(*goal)))
    return lax.ppermute(block, ("dp", "ctx"), route)


def to_core(x, y, z, c):
    return (x, y, z, 1 - c)


def to_y(x, y, z, c):
    return (x, y - 1 if c == 0 else y + 1, z, c)


def to_x(x, y, z, c):
    return (x - 1 if c == 0 else x + 1, y, z, c)


def to_z1(x, y, z, c):
    return (x, y, z ^ 1, c)


def to_z3(x, y, z, c):
    return (x, y, z ^ 3, c)


def to_y2(x, y, z, c):
    return (x, y + 2, z, c)


def held(*arrays):
    return [pltpu.with_memory_space_constraint(a, pltpu.VMEM) for a in arrays]


def far(*arrays):
    return [pltpu.with_memory_space_constraint(a, pltpu.HBM) for a in arrays]


HELD = pl.BlockSpec(memory_space=pltpu.VMEM)
SCALARS = pl.BlockSpec(memory_space=pltpu.SMEM)
FAR = pl.BlockSpec(memory_space=pltpu.HBM)


def params(mib):
    return pltpu.CompilerParams(vmem_limit_bytes=mib << 20)


def stage_kernel(x_own, x_oth, x_all, sem):
    copies = [pltpu.make_async_copy(x, x_all.at[pl.ds(g * TOK, TOK)], sem.at[g]) for g, x in enumerate((x_own, x_oth))]
    for copy in copies:
        copy.start()
    for copy in copies:
        copy.wait()


def stage(x_own, x_oth):
    return pl.pallas_call(
        stage_kernel,
        out_shape=pltpu.VMEM((ROWS, x_own.shape[1]), x_own.dtype),
        in_specs=[FAR, FAR],
        out_specs=HELD,
        scratch_shapes=[pltpu.SemaphoreType.DMA((2,))],
        compiler_params=params(6),
        name="stage",
    )(*far(x_own, x_oth))


def payload_kernel(block, w, out, sem):
    core = lax.axis_index("ctx") % 2
    half = w.shape[0] // 2
    rows = pl.ds(pl.multiple_of(core * half, half), half)
    copy = pltpu.make_async_copy(w.at[rows, pl.ds(pl.multiple_of(block() * WB, HD), WB)], out, sem.at[0])
    copy.start()
    copy.wait()


def payload(block, w):
    return pl.pallas_call(
        lambda *refs: payload_kernel(block, *refs),
        out_shape=pltpu.VMEM((w.shape[0] // 2, WB), w.dtype),
        in_specs=[FAR],
        out_specs=HELD,
        scratch_shapes=[pltpu.SemaphoreType.DMA((1,))],
        compiler_params=params(6),
    )(*far(w))


def first_block():
    odd = (lax.axis_index("ctx") // 16) % 2
    return 2 - 2 * lax.rem(lax.axis_index("dp") + odd, 2)


CUT2, CUT3 = ROWS >> 2, (ROWS >> 2) + (ROWS >> 3)


def proj_kernel(remote, slot, for_keys, meta, x_all, w_loc, *rest):
    halves = rest[: 2 * remote]
    outs, (wbuf, acc, wsem) = rest[2 * remote : -3], rest[-3:]
    chunks = w_loc.shape[0] // KC
    core = meta[META_CORE]
    src = meta[slot]
    col = pl.multiple_of(meta[slot + 1] * WB, HD)
    for i in range(chunks):
        rows = pl.ds(i * KC, KC)

        @pl.when(src == 0)
        def _():
            pltpu.make_async_copy(w_loc.at[rows, pl.ds(col, WB)], wbuf.at[rows], wsem.at[i]).start()

        part = i * 2 // chunks
        low = pl.ds((i - part * (chunks // 2)) * KC, KC)
        for r in range(remote):
            for own in range(2):

                @pl.when((src == r + 1) & ((core == part) if own else (core != part)))
                def _():
                    pltpu.make_async_copy(halves[2 * r + 1 - own].at[low], wbuf.at[rows], wsem.at[i]).start()

    for i in range(chunks):
        rows = pl.ds(i * KC, KC)
        pltpu.make_async_copy(w_loc.at[rows, pl.ds(0, WB)], wbuf.at[rows], wsem.at[i]).wait()
        for g in range(2):
            span = pl.ds(g * TOK, TOK)
            got = jnp.dot(x_all[span, rows], wbuf[rows], preferred_element_type=jnp.float32)
            for h in range(HH):
                piece = got[:, h * HD : (h + 1) * HD]
                if i > 0:
                    piece = acc[h, span] + piece
                acc[h, span] = piece
                if i == chunks - 1:
                    outs[0][span, pl.ds(h * HD, HD)] = piece.astype(jnp.bfloat16)
    for h in range(HH):
        cols = pl.ds(h * HD, HD)
        kept = [
            acc[h, pl.ds(meta[META_OFF + j * HH + h], ROWS >> j, stride=1 << j), :].astype(jnp.bfloat16)
            for j in range(1, LEVELS)
        ]
        outs[1][:, cols] = kept[0]
        outs[2][pl.ds(0, CUT2), cols] = kept[1]
        outs[2][pl.ds(CUT2, ROWS >> 3), cols] = kept[2]
        if for_keys:
            outs[2][pl.ds(CUT3, ROWS >> 3), cols] = kept[2]
            outs[3][:, cols] = kept[2]


def project(meta, slot, x_all, w_loc, remotes, for_keys):
    depth = w_loc.shape[0]
    flat = [half for pair in remotes for half in pair]
    shapes = [(ROWS, WB), (ROWS >> 1, WB)] + ([(ROWS >> 1, WB), (ROWS >> 3, WB)] if for_keys else [(CUT3, WB)])
    return pl.pallas_call(
        lambda *refs: proj_kernel(len(remotes), slot, for_keys, *refs),
        out_shape=[pltpu.VMEM(s, jnp.bfloat16) for s in shapes],
        in_specs=[SCALARS, HELD] + [FAR] * (1 + len(flat)),
        out_specs=[HELD] * len(shapes),
        scratch_shapes=[
            pltpu.VMEM((depth, WB), jnp.bfloat16),
            pltpu.VMEM((HH, ROWS, HD), jnp.float32),
            pltpu.SemaphoreType.DMA((depth // KC,)),
        ],
        compiler_params=params(16),
        cost_estimate=pl.CostEstimate(
            flops=2 * ROWS * depth * WB, transcendentals=0, bytes_accessed=2 * (ROWS * depth + depth * WB + 2 * ROWS * WB)
        ),
    )(meta, *held(x_all), *far(w_loc, *flat))


def softmax_rows(q, keys, values, factor):
    scores = [lax.dot_general(q, k, (((1,), (1,)), ((), ())), preferred_element_type=jnp.float32) for k in keys]
    top = scores[0].max(axis=1, keepdims=True)
    for s in scores[1:]:
        top = jnp.maximum(top, s.max(axis=1, keepdims=True))
    total, blend = 0.0, 0.0
    for s, v in zip(scores, values):
        e = jnp.exp2((s - top) * factor)
        total = total + e.sum(axis=1, keepdims=True)
        blend = blend + jnp.dot(e.astype(jnp.bfloat16), v, preferred_element_type=jnp.float32)
    return blend, top * factor, total


def pack(top, total):
    lane = lax.broadcasted_iota(jnp.int32, (1, HD), 1)
    return jnp.where(lane == 0, top, total)


def merge(acc_ref, ml_ref, where, blend, top, total):
    old = ml_ref[where]
    old_top, old_total = old[:, 0:1], old[:, 1:2]
    newest = jnp.maximum(old_top, top)
    former, fresh = jnp.exp2(old_top - newest), jnp.exp2(top - newest)
    acc_ref[where] = acc_ref[where] * former + blend * fresh
    ml_ref[where] = pack(newest, old_total * former + total * fresh)


def choose(meta, firsts, seconds, cut, cols):
    f_is_k = jnp.full((1, 1), meta[META_FK], jnp.int32) == 1
    keys, values = [], []
    for f_ref, s_ref in zip(firsts, seconds):
        f, s = f_ref[cut, cols], s_ref[cut, cols]
        keys.append(jnp.where(f_is_k, f, s))
        values.append(jnp.where(f_is_k, s, f))
    return keys, values


def level0_kernel(factor, meta, q_ref, f_ref, s_ref, acc_ref, ml_ref):
    for h in range(HH):
        cols = pl.ds(h * HD, HD)
        keys, values = choose(meta, [f_ref], [s_ref], slice(None), cols)
        for start in range(0, ROWS, TOK):
            blend, top, total = softmax_rows(q_ref[pl.ds(start, TOK), cols], keys, values, factor)
            acc_ref[h, pl.ds(start, TOK), :] = blend
            ml_ref[h, pl.ds(start, TOK), :] = pack(top, total)


def level1_kernel(factor, meta, q_ref, f0, f1, s0, s1, _acc, _ml, acc_ref, ml_ref):
    for h in range(HH):
        cols = pl.ds(h * HD, HD)
        keys, values = choose(meta, [f0, f1], [s0, s1], slice(None), cols)
        where = (h, pl.ds(meta[META_OFF + HH + h], TOK, stride=2), slice(None))
        merge(acc_ref, ml_ref, where, *softmax_rows(q_ref[:, cols], keys, values, factor))


def level23_kernel(factor, meta, q_ref, f0, f1, f2, f3, s0, s1, s2, s3, _acc, _ml, own_ref, oth_ref, acc, ml):
    for h in range(HH):
        cols = pl.ds(h * HD, HD)
        for level, low, rows in ((2, 0, CUT2), (3, CUT2, ROWS >> 3)):
            cut = slice(0, CUT2) if level == 2 else slice(CUT2, ROWS >> 1)
            keys, values = choose(meta, [f0, f1, f2, f3], [s0, s1, s2, s3], cut, cols)
            where = (h, pl.ds(meta[META_OFF + level * HH + h], rows, stride=1 << level), slice(None))
            merge(acc, ml, where, *softmax_rows(q_ref[pl.ds(low, rows), cols], keys, values, factor))
        share = acc[h] * (1.0 / ml[h][:, 1:2])
        own_ref[:, cols] = share[:TOK].astype(jnp.bfloat16)
        oth_ref[:, cols] = share[TOK:].astype(jnp.bfloat16)


STATE = [((HH, ROWS, HD), jnp.float32)] * 2


def attend(kernel, meta, arrays, outs, rows, alias=None):
    factor = HD ** (-0.5) * LOG2E
    return pl.pallas_call(
        lambda *refs: kernel(factor, *refs),
        out_shape=[pltpu.VMEM(*o) for o in outs],
        in_specs=[SCALARS] + [HELD] * len(arrays),
        out_specs=[HELD] * len(outs),
        input_output_aliases=alias or {},
        compiler_params=params(20),
        cost_estimate=pl.CostEstimate(
            flops=4 * rows * ROWS * WB, transcendentals=rows * ROWS * HH, bytes_accessed=2 * (rows + 2 * ROWS) * WB
        ),
    )(meta, *held(*arrays))


def tile_of(t, core_rows, w_loc, rem):
    cols = pl.ds((t % 2) * WB, WB)
    return w_loc[core_rows, cols] if t < 2 else rem[:, cols]


def out_own_kernel(meta, att, w_loc, rem, part):
    rows = pl.ds(pl.multiple_of(meta[META_CORE] * WB, HD), WB)
    for t in range(4):
        part[t] = jnp.dot(att[...], tile_of(t, rows, w_loc, rem), preferred_element_type=jnp.float32)


def out_oth_kernel(meta, att, w_loc, rem, part, out, buf, sem):
    rows = pl.ds(pl.multiple_of((1 - meta[META_CORE]) * WB, HD), WB)
    d = meta[META_DP]
    copies = []
    for t in range(4):
        got = part[t] + jnp.dot(att[...], tile_of(t, rows, w_loc, rem), preferred_element_type=jnp.float32)
        buf[t] = got.astype(jnp.bfloat16)
        col = (d if t < 2 else 1 - d) * (2 * WB) + (t % 2) * WB
        copies.append(pltpu.make_async_copy(buf.at[t], out.at[:, pl.ds(pl.multiple_of(col, HD), WB)], sem.at[t]))
        copies[-1].start()
    for copy in copies:
        copy.wait()


def out_project(kernel, meta, arrays, out_shape, out_spec, scratch):
    return pl.pallas_call(
        kernel,
        out_shape=out_shape,
        in_specs=[SCALARS] + [HELD] * len(arrays),
        out_specs=out_spec,
        scratch_shapes=scratch,
        compiler_params=params(16),
        cost_estimate=pl.CostEstimate(flops=8 * TOK * WB * WB, transcendentals=0, bytes_accessed=8 * WB * WB + 8 * TOK * WB),
    )(meta, *held(*arrays))


def local(tokens, qkv_weight, out_weight, offsets):
    d = lax.axis_index("dp")
    ctx = lax.axis_index("ctx")
    core = ctx & 1
    odd = (ctx >> 4) & 1
    depth = qkv_weight.shape[0]

    pick = lambda a0, a1, b0, b1: jnp.where(d == 0, jnp.where(core == 0, a0, a1), jnp.where(core == 0, b0, b1))
    f_src, f_blk = pick(0, 1, 0, 0), pick(2, 0, 1, 0)
    s_src, s_blk = pick(3, 2, 1 + odd, 0), pick(0, 0, 0, 2)
    q_src, q_blk = pick(0, 0, 2 - odd, 3), pick(0, 1, 0, 0)
    f_is_k = pick(1, 1 - odd, 0, 1)
    zero = jnp.zeros((), jnp.int32)
    heads = lax.dynamic_slice(offsets, (0, core * HH), (LEVELS, HH)).reshape(-1)
    meta = jnp.concatenate(
        [jnp.stack([core, f_src, f_blk, s_src, s_blk, q_src, q_blk, f_is_k, d] + [zero] * 7).astype(jnp.int32), heads]
    )

    x_own = tokens.reshape(TOK, depth)
    first_own = send(payload(first_block, qkv_weight), to_y)
    x_oth = send(x_own, to_core)
    side_own = send(payload(lambda: 1, qkv_weight), to_y)
    x_all = stage(x_own, x_oth)
    first_fwd = send(first_own, to_core)
    relay_own = send(first_own, to_x)
    relay_fwd = send(relay_own, to_core)
    side_fwd = send(side_own, to_core)

    def gather(block):
        far = send(block[3], to_y2)
        joined = lax.dynamic_update_slice(block[2], far, (CUT3, 0))
        pair = send(joined, to_z1)
        ring = send(joined, to_z3)
        relay = send(pair, to_z3)
        return (joined, pair, ring, relay), send(block[1], to_z1)

    first = project(meta, META_FSRC, x_all, qkv_weight, [(first_own, first_fwd)], True)
    f23, f1_pair = gather(first)
    everything = [(first_own, first_fwd), (relay_own, relay_fwd), (side_own, side_fwd)]
    second = project(meta, META_SSRC, x_all, qkv_weight, everything, True)
    s23, s1_pair = gather(second)
    queries = project(meta, META_QSRC, x_all, qkv_weight, everything, False)

    w_own = lax.dynamic_slice(out_weight, (core * WB, zero), (WB, out_weight.shape[1]))
    rem_own = send(w_own, to_y)
    rem_oth = send(rem_own, to_core)

    state = attend(level0_kernel, meta, [queries[0], first[0], second[0]], STATE, ROWS)
    arrays = [queries[1], first[1], f1_pair, second[1], s1_pair, *state]
    state = attend(level1_kernel, meta, arrays, STATE, ROWS >> 1, {6: 0, 7: 1})
    arrays = [queries[2], *f23, *s23, *state]
    outs = [((TOK, WB), jnp.bfloat16)] * 2 + STATE
    att, att_send, _, _ = attend(level23_kernel, meta, arrays, outs, CUT3, {10: 2, 11: 3})
    att_oth = send(att_send, to_core)
    part = out_project(
        out_own_kernel, meta, [att, out_weight, rem_own], pltpu.VMEM((4, TOK, WB), jnp.float32), HELD, []
    )
    mixed = out_project(
        out_oth_kernel,
        meta,
        [att_oth, out_weight, rem_oth, part],
        jax.ShapeDtypeStruct((TOK, 4 * WB), jnp.bfloat16),
        FAR,
        [pltpu.VMEM((4, TOK, WB), jnp.bfloat16), pltpu.SemaphoreType.DMA((4,))],
    )
    return mixed.reshape(1, TOK, mixed.shape[1])


def solution(mesh):
    in_specs = (P("dp", "ctx", None), P(None, "dp"), P(None, "dp"), P())
    out_specs = P("dp", "ctx", None)

    return jax.shard_map(local, mesh=mesh, in_specs=in_specs, out_specs=out_specs, check_vma=False)
```

```python
import jax
import jax.numpy as jnp
from jax import lax
from jax.experimental import pallas as pl
from jax.experimental.pallas import tpu as pltpu
from jax.sharding import PartitionSpec as P


TOK = 384
ROWS = 2 * TOK
HD = 128
HH = 5
WB = HH * HD
LEVELS = 4
KC = 1280
LOG2E = 1.4426950408889634

META_CORE, META_FSRC, META_FBLK, META_SSRC, META_SBLK, META_QSRC, META_QBLK, META_FK, META_DP = range(9)
META_OFF = 16


def lin(x, y, z, c):
    return (y % 2) * 64 + (((x % 4) * 2 + (y % 4) // 2) * 4 + z % 4) * 2 + c


def send(block, target):
    route = []
    for x in range(4):
        for y in range(4):
            for z in range(4):
                for c in range(2):
                    goal = target(x, y, z, c)
                    if goal is not None:
                        route.append((lin(x, y, z, c), lin(*goal)))
    return lax.ppermute(block, ("dp", "ctx"), route)


def to_core(x, y, z, c):
    return (x, y, z, 1 - c)


def to_y(x, y, z, c):
    return (x, y - 1 if c == 0 else y + 1, z, c)


def to_x(x, y, z, c):
    return (x - 1 if c == 0 else x + 1, y, z, c)


def to_z1(x, y, z, c):
    return (x, y, z ^ 1, c)


def to_z3(x, y, z, c):
    return (x, y, z ^ 3, c)


def to_y2(x, y, z, c):
    return (x, y + 2, z, c)


def held(*arrays):
    return [pltpu.with_memory_space_constraint(a, pltpu.VMEM) for a in arrays]


def far(*arrays):
    return [pltpu.with_memory_space_constraint(a, pltpu.HBM) for a in arrays]


HELD = pl.BlockSpec(memory_space=pltpu.VMEM)
SCALARS = pl.BlockSpec(memory_space=pltpu.SMEM)
FAR = pl.BlockSpec(memory_space=pltpu.HBM)


def params(mib):
    return pltpu.CompilerParams(vmem_limit_bytes=mib << 20)


def scalars_kernel(offsets, meta):
    d = lax.axis_index("dp")
    ctx = lax.axis_index("ctx")
    core = lax.rem(ctx, 2)
    odd = lax.rem(ctx // 16, 2)
    place = 2 * d + core

    def pick(*by_place):
        got = jnp.int32(by_place[3])
        for n in range(3):
            got = jnp.where(place == n, by_place[n], got)
        return got

    meta[META_CORE] = core
    meta[META_DP] = d
    meta[META_FSRC], meta[META_FBLK] = pick(0, 1, 0, 0), pick(2, 0, 1, 0)
    meta[META_SSRC], meta[META_SBLK] = pick(3, 2, 1 + odd, 0), pick(0, 0, 0, 2)
    meta[META_QSRC], meta[META_QBLK] = pick(0, 0, 2 - odd, 3), pick(0, 1, 0, 0)
    meta[META_FK] = pick(1, 1 - odd, 0, 1)
    for n in range(9, META_OFF):
        meta[n] = 0
    for j in range(LEVELS):
        for h in range(HH):
            meta[META_OFF + j * HH + h] = jnp.where(core == 0, offsets[j, h], offsets[j, HH + h])


def stage_kernel(x_own, x_oth, x_all, sem):
    copies = [pltpu.make_async_copy(x, x_all.at[pl.ds(g * TOK, TOK)], sem.at[g]) for g, x in enumerate((x_own, x_oth))]
    for copy in copies:
        copy.start()
    for copy in copies:
        copy.wait()


def stage(x_own, x_oth):
    return pl.pallas_call(
        stage_kernel,
        out_shape=pltpu.VMEM((ROWS, x_own.shape[1]), x_own.dtype),
        in_specs=[FAR, FAR],
        out_specs=HELD,
        scratch_shapes=[pltpu.SemaphoreType.DMA((2,))],
        compiler_params=params(6),
        name="stage",
    )(*far(x_own, x_oth))


def join_kernel(far_rows, _block, out):
    out[pl.ds(CUT3, ROWS >> 3), :] = far_rows[...]


def join(block, far_rows):
    return pl.pallas_call(
        join_kernel,
        out_shape=pltpu.VMEM(block.shape, block.dtype),
        in_specs=[HELD, HELD],
        out_specs=HELD,
        input_output_aliases={1: 0},
        compiler_params=params(3),
    )(*held(far_rows, block))


def collect_kernel(*refs):
    for n, ref in enumerate(refs[:-1]):
        refs[-1][pl.ds(n * (ROWS >> 3), ROWS >> 3), :] = ref[pl.ds(CUT2, ROWS >> 3), :]


def collect(blocks):
    return pl.pallas_call(
        collect_kernel,
        out_shape=pltpu.VMEM((len(blocks) * (ROWS >> 3), WB), blocks[0].dtype),
        in_specs=[HELD] * len(blocks),
        out_specs=HELD,
        compiler_params=params(3),
    )(*held(*blocks))


def payload_kernel(block, w, out, sem):
    core = lax.rem(lax.axis_index("ctx"), 2)
    half = w.shape[0] // 2
    rows = pl.ds(pl.multiple_of(core * half, half), half)
    source = w.at[rows] if block is None else w.at[rows, pl.ds(pl.multiple_of(block() * WB, HD), WB)]
    copy = pltpu.make_async_copy(source, out, sem.at[0])
    copy.start()
    copy.wait()


def payload(block, w):
    return pl.pallas_call(
        lambda *refs: payload_kernel(block, *refs),
        out_shape=pltpu.VMEM((w.shape[0] // 2, w.shape[1] if block is None else WB), w.dtype),
        in_specs=[FAR],
        out_specs=HELD,
        scratch_shapes=[pltpu.SemaphoreType.DMA((1,))],
        compiler_params=params(6),
    )(*far(w))


def first_block():
    odd = (lax.axis_index("ctx") // 16) % 2
    return 2 - 2 * lax.rem(lax.axis_index("dp") + odd, 2)


CUT2, CUT3 = ROWS >> 2, (ROWS >> 2) + (ROWS >> 3)


def proj_kernel(remote, slot, for_keys, meta, x_all, w_loc, *rest):
    halves = rest[: 2 * remote]
    outs, (wbuf, acc, wsem) = rest[2 * remote : -3], rest[-3:]
    chunks = w_loc.shape[0] // KC
    core = meta[META_CORE]
    src = meta[slot]
    col = pl.multiple_of(meta[slot + 1] * WB, HD)
    for i in range(chunks):
        rows = pl.ds(i * KC, KC)

        @pl.when(src == 0)
        def _():
            pltpu.make_async_copy(w_loc.at[rows, pl.ds(col, WB)], wbuf.at[rows], wsem.at[i]).start()

        part = i * 2 // chunks
        low = pl.ds((i - part * (chunks // 2)) * KC, KC)
        for r in range(remote):
            for own in range(2):

                @pl.when((src == r + 1) & ((core == part) if own else (core != part)))
                def _():
                    pltpu.make_async_copy(halves[2 * r + 1 - own].at[low], wbuf.at[rows], wsem.at[i]).start()

    for i in range(chunks):
        rows = pl.ds(i * KC, KC)
        pltpu.make_async_copy(w_loc.at[rows, pl.ds(0, WB)], wbuf.at[rows], wsem.at[i]).wait()
        for g in range(2):
            span = pl.ds(g * TOK, TOK)
            got = jnp.dot(x_all[span, rows], wbuf[rows], preferred_element_type=jnp.float32)
            for h in range(HH):
                piece = got[:, h * HD : (h + 1) * HD]
                if i > 0:
                    piece = acc[h, span] + piece
                acc[h, span] = piece
                if i == chunks - 1:
                    outs[0][span, pl.ds(h * HD, HD)] = piece.astype(jnp.bfloat16)
    for h in range(HH):
        cols = pl.ds(h * HD, HD)
        kept = [
            acc[h, pl.ds(meta[META_OFF + j * HH + h], ROWS >> j, stride=1 << j), :].astype(jnp.bfloat16)
            for j in range(1, LEVELS)
        ]
        outs[1][:, cols] = kept[0]
        outs[2][pl.ds(0, CUT2), cols] = kept[1]
        outs[2][pl.ds(CUT2, ROWS >> 3), cols] = kept[2]
        if for_keys:
            outs[2][pl.ds(CUT3, ROWS >> 3), cols] = kept[2]
            outs[3][:, cols] = kept[2]


def project(meta, slot, x_all, w_loc, remotes, for_keys):
    depth = w_loc.shape[0]
    flat = [half for pair in remotes for half in pair]
    shapes = [(ROWS, WB), (ROWS >> 1, WB)] + ([(ROWS >> 1, WB), (ROWS >> 3, WB)] if for_keys else [(CUT3, WB)])
    return pl.pallas_call(
        lambda *refs: proj_kernel(len(remotes), slot, for_keys, *refs),
        out_shape=[pltpu.VMEM(s, jnp.bfloat16) for s in shapes],
        in_specs=[SCALARS, HELD, FAR] + [HELD] * len(flat),
        out_specs=[HELD] * len(shapes),
        scratch_shapes=[
            pltpu.VMEM((depth, WB), jnp.bfloat16),
            pltpu.VMEM((HH, ROWS, HD), jnp.float32),
            pltpu.SemaphoreType.DMA((depth // KC,)),
        ],
        compiler_params=params(16),
        cost_estimate=pl.CostEstimate(
            flops=2 * ROWS * depth * WB, transcendentals=0, bytes_accessed=2 * (ROWS * depth + depth * WB + 2 * ROWS * WB)
        ),
    )(meta, *held(x_all), *far(w_loc), *held(*flat))


def softmax_rows(q, keys, values, factor):
    scores = [lax.dot_general(q, k, (((1,), (1,)), ((), ())), preferred_element_type=jnp.float32) for k in keys]
    top = scores[0].max(axis=1, keepdims=True)
    for s in scores[1:]:
        top = jnp.maximum(top, s.max(axis=1, keepdims=True))
    total, blend = 0.0, 0.0
    for s, v in zip(scores, values):
        e = jnp.exp2((s - top) * factor)
        total = total + e.sum(axis=1, keepdims=True)
        blend = blend + jnp.dot(e.astype(jnp.bfloat16), v, preferred_element_type=jnp.float32)
    return blend, top * factor, total


def pack(top, total):
    lane = lax.broadcasted_iota(jnp.int32, (1, HD), 1)
    return jnp.where(lane == 0, top, total)


def merge(acc_ref, ml_ref, where, blend, top, total):
    old = ml_ref[where]
    old_top, old_total = old[:, 0:1], old[:, 1:2]
    newest = jnp.maximum(old_top, top)
    former, fresh = jnp.exp2(old_top - newest), jnp.exp2(top - newest)
    acc_ref[where] = acc_ref[where] * former + blend * fresh
    ml_ref[where] = pack(newest, old_total * former + total * fresh)


def choose(meta, firsts, seconds):
    f_is_k = jnp.full((1, 1), meta[META_FK], jnp.int32) == 1
    f = firsts[0] if len(firsts) == 1 else jnp.concatenate(firsts, axis=0)
    s = seconds[0] if len(seconds) == 1 else jnp.concatenate(seconds, axis=0)
    return [jnp.where(f_is_k, f, s)], [jnp.where(f_is_k, s, f)]


def level0_kernel(factor, meta, q_ref, f_ref, s_ref, acc_ref, ml_ref):
    for h in range(HH):
        cols = pl.ds(h * HD, HD)
        keys, values = choose(meta, [f_ref[:, cols]], [s_ref[:, cols]])
        for start in range(0, ROWS, TOK):
            blend, top, total = softmax_rows(q_ref[pl.ds(start, TOK), cols], keys, values, factor)
            acc_ref[h, pl.ds(start, TOK), :] = blend
            ml_ref[h, pl.ds(start, TOK), :] = pack(top, total)


def level1_kernel(factor, meta, q_ref, f0, f1, s0, s1, _acc, _ml, acc_ref, ml_ref):
    for h in range(HH):
        cols = pl.ds(h * HD, HD)
        keys, values = choose(meta, [f0[:, cols], f1[:, cols]], [s0[:, cols], s1[:, cols]])
        where = (h, pl.ds(meta[META_OFF + HH + h], TOK, stride=2), slice(None))
        merge(acc_ref, ml_ref, where, *softmax_rows(q_ref[:, cols], keys, values, factor))


def level23_kernel(factor, meta, q_ref, *refs):
    fs, f_far, ss, (own_ref, oth_ref, acc, ml) = refs[:4], refs[4], refs[5:9], refs[11:]
    third = ROWS >> 3
    for h in range(HH):
        cols = pl.ds(h * HD, HD)
        for level, low, rows in ((2, 0, CUT2), (3, CUT2, third)):
            if level == 2:
                firsts, seconds = [f[:CUT2, cols] for f in fs], [s[:CUT2, cols] for s in ss]
            else:
                firsts = [r for n, f in enumerate(fs) for r in (f[CUT2:, cols], f_far[pl.ds(n * third, third), cols])]
                seconds = [s[CUT2:, cols] for s in ss]
            keys, values = choose(meta, firsts, seconds)
            where = (h, pl.ds(meta[META_OFF + level * HH + h], rows, stride=1 << level), slice(None))
            merge(acc, ml, where, *softmax_rows(q_ref[pl.ds(low, rows), cols], keys, values, factor))
        share = acc[h] * (1.0 / ml[h][:, 1:2])
        own_ref[:, cols] = share[:TOK].astype(jnp.bfloat16)
        oth_ref[:, cols] = share[TOK:].astype(jnp.bfloat16)


STATE = [((HH, ROWS, HD), jnp.float32)] * 2


def attend(kernel, meta, arrays, outs, rows, alias=None):
    factor = HD ** (-0.5) * LOG2E
    return pl.pallas_call(
        lambda *refs: kernel(factor, *refs),
        out_shape=[pltpu.VMEM(*o) for o in outs],
        in_specs=[SCALARS] + [HELD] * len(arrays),
        out_specs=[HELD] * len(outs),
        input_output_aliases=alias or {},
        compiler_params=params(20),
        cost_estimate=pl.CostEstimate(
            flops=4 * rows * ROWS * WB, transcendentals=rows * ROWS * HH, bytes_accessed=2 * (rows + 2 * ROWS) * WB
        ),
    )(meta, *held(*arrays))


def tile_of(t, core_rows, w_loc, rem):
    cols = pl.ds((t % 2) * WB, WB)
    return w_loc[core_rows, cols] if t < 2 else rem[:, cols]


def out_own_kernel(meta, att, w_loc, rem, part):
    rows = pl.ds(pl.multiple_of(meta[META_CORE] * WB, HD), WB)
    for t in range(4):
        part[t] = jnp.dot(att[...], tile_of(t, rows, w_loc, rem), preferred_element_type=jnp.float32)


def out_oth_kernel(meta, att, w_loc, rem, part, out, buf, sem):
    rows = pl.ds(pl.multiple_of((1 - meta[META_CORE]) * WB, HD), WB)
    d = meta[META_DP]
    copies = []
    for t in range(4):
        got = part[t] + jnp.dot(att[...], tile_of(t, rows, w_loc, rem), preferred_element_type=jnp.float32)
        buf[t] = got.astype(jnp.bfloat16)
        col = (d if t < 2 else 1 - d) * (2 * WB) + (t % 2) * WB
        copies.append(pltpu.make_async_copy(buf.at[t], out.at[:, pl.ds(pl.multiple_of(col, HD), WB)], sem.at[t]))
        copies[-1].start()
    for copy in copies:
        copy.wait()


def out_project(kernel, meta, arrays, out_shape, out_spec, scratch):
    return pl.pallas_call(
        kernel,
        out_shape=out_shape,
        in_specs=[SCALARS] + [HELD] * len(arrays),
        out_specs=out_spec,
        scratch_shapes=scratch,
        compiler_params=params(16),
        cost_estimate=pl.CostEstimate(flops=8 * TOK * WB * WB, transcendentals=0, bytes_accessed=8 * WB * WB + 8 * TOK * WB),
    )(meta, *held(*arrays))


def local(tokens, qkv_weight, out_weight, offsets):
    depth = qkv_weight.shape[0]
    meta = pl.pallas_call(
        scalars_kernel,
        out_shape=jax.ShapeDtypeStruct((META_OFF + LEVELS * HH,), jnp.int32),
        in_specs=[SCALARS],
        out_specs=SCALARS,
        compiler_params=params(1),
        name="scalars",
    )(offsets)

    x_own = tokens.reshape(TOK, depth)
    first_own = send(payload(first_block, qkv_weight), to_y)
    x_oth = send(x_own, to_core)
    side_own = send(payload(lambda: 1, qkv_weight), to_y)
    x_all = stage(x_own, x_oth)
    first_fwd = send(first_own, to_core)
    relay_own = send(first_own, to_x)
    relay_fwd = send(relay_own, to_core)
    side_fwd = send(side_own, to_core)

    def along_z(rows):
        pair = send(rows, to_z1)
        ring = send(rows, to_z3)
        return [rows, pair, ring, send(pair, to_z3)]

    def gather(block):
        far = send(block[3], to_y2)
        joined = join(block[2], far)
        return along_z(joined), send(block[1], to_z1)

    first = project(meta, META_FSRC, x_all, qkv_weight, [(first_own, first_fwd)], False)
    f23 = along_z(first[2])
    f1_pair = send(first[1], to_z1)
    f3_far = send(collect(f23), to_y2)
    everything = [(first_own, first_fwd), (relay_own, relay_fwd), (side_own, side_fwd)]
    second = project(meta, META_SSRC, x_all, qkv_weight, everything, True)
    s23, s1_pair = gather(second)
    queries = project(meta, META_QSRC, x_all, qkv_weight, everything, False)

    rem_own = send(payload(None, out_weight), to_y)
    rem_oth = send(rem_own, to_core)

    state = attend(level0_kernel, meta, [queries[0], first[0], second[0]], STATE, ROWS)
    arrays = [queries[1], first[1], f1_pair, second[1], s1_pair, *state]
    state = attend(level1_kernel, meta, arrays, STATE, ROWS >> 1, {6: 0, 7: 1})
    arrays = [queries[2], *f23, f3_far, *s23, *state]
    outs = [((TOK, WB), jnp.bfloat16)] * 2 + STATE
    att, att_send, _, _ = attend(level23_kernel, meta, arrays, outs, CUT3, {11: 2, 12: 3})
    att_oth = send(att_send, to_core)
    part = out_project(
        out_own_kernel, meta, [att, out_weight, rem_own], pltpu.VMEM((4, TOK, WB), jnp.float32), HELD, []
    )
    mixed = out_project(
        out_oth_kernel,
        meta,
        [att_oth, out_weight, rem_oth, part],
        jax.ShapeDtypeStruct((TOK, 4 * WB), jnp.bfloat16),
        FAR,
        [pltpu.VMEM((4, TOK, WB), jnp.bfloat16), pltpu.SemaphoreType.DMA((4,))],
    )
    return mixed.reshape(1, TOK, mixed.shape[1])


def solution(mesh):
    in_specs = (P("dp", "ctx", None), P(None, "dp"), P(None, "dp"), P())
    out_specs = P("dp", "ctx", None)

    return jax.shard_map(local, mesh=mesh, in_specs=in_specs, out_specs=out_specs, check_vma=False)
```

```python
import jax
import jax.numpy as jnp
from jax import lax
from jax.experimental import pallas as pl
from jax.experimental.pallas import tpu as pltpu
from jax.sharding import PartitionSpec as P


TOK = 384
ROWS = 2 * TOK
HD = 128
HH = 5
WB = HH * HD
LEVELS = 4
LOG2E = 1.4426950408889634

META_CORE, META_FSRC, META_FBLK, META_SSRC, META_SBLK, META_QSRC, META_QBLK, META_FK, META_DP = range(9)
META_OFF = 16


def lin(x, y, z, c):
    return (y % 2) * 64 + (((x % 4) * 2 + (y % 4) // 2) * 4 + z % 4) * 2 + c


def send(block, target):
    route = []
    for x in range(4):
        for y in range(4):
            for z in range(4):
                for c in range(2):
                    goal = target(x, y, z, c)
                    if goal is not None:
                        route.append((lin(x, y, z, c), lin(*goal)))
    return lax.ppermute(block, ("dp", "ctx"), route)


def to_core(x, y, z, c):
    return (x, y, z, 1 - c)


def to_y(x, y, z, c):
    return (x, y - 1 if c == 0 else y + 1, z, c)


def to_x(x, y, z, c):
    return (x - 1 if c == 0 else x + 1, y, z, c)


def to_z1(x, y, z, c):
    return (x, y, z ^ 1, c)


def to_z3(x, y, z, c):
    return (x, y, z ^ 3, c)


def to_y2(x, y, z, c):
    return (x, y + 2, z, c)


def held(*arrays):
    return [pltpu.with_memory_space_constraint(a, pltpu.VMEM) for a in arrays]


def far(*arrays):
    return [pltpu.with_memory_space_constraint(a, pltpu.HBM) for a in arrays]


HELD = pl.BlockSpec(memory_space=pltpu.VMEM)
SCALARS = pl.BlockSpec(memory_space=pltpu.SMEM)
FAR = pl.BlockSpec(memory_space=pltpu.HBM)


def params(mib):
    return pltpu.CompilerParams(vmem_limit_bytes=mib << 20)


def scalars_kernel(offsets, meta):
    d = lax.axis_index("dp")
    ctx = lax.axis_index("ctx")
    core = lax.rem(ctx, 2)
    odd = lax.rem(ctx // 16, 2)
    place = 2 * d + core

    def pick(*by_place):
        got = jnp.int32(by_place[3])
        for n in range(3):
            got = jnp.where(place == n, by_place[n], got)
        return got

    meta[META_CORE] = core
    meta[META_DP] = d
    meta[META_FSRC], meta[META_FBLK] = pick(0, 1, 0, 0), pick(2, 0, 1, 0)
    meta[META_SSRC], meta[META_SBLK] = pick(3, 2, 1 + odd, 0), pick(0, 0, 0, 2)
    meta[META_QSRC], meta[META_QBLK] = pick(0, 0, 2 - odd, 3), pick(0, 1, 0, 0)
    meta[META_FK] = pick(1, 1 - odd, 0, 1)
    for n in range(9, META_OFF):
        meta[n] = 0
    for j in range(LEVELS):
        for h in range(HH):
            meta[META_OFF + j * HH + h] = jnp.where(core == 0, offsets[j, h], offsets[j, HH + h])


def stage_kernel(x_own, x_oth, x_all, sem):
    copies = [pltpu.make_async_copy(x, x_all.at[pl.ds(g * TOK, TOK)], sem.at[g]) for g, x in enumerate((x_own, x_oth))]
    for copy in copies:
        copy.start()
    for copy in copies:
        copy.wait()


def stage(x_own, x_oth):
    return pl.pallas_call(
        stage_kernel,
        out_shape=pltpu.VMEM((ROWS, x_own.shape[1]), x_own.dtype),
        in_specs=[FAR, FAR],
        out_specs=HELD,
        scratch_shapes=[pltpu.SemaphoreType.DMA((2,))],
        compiler_params=params(6),
        name="stage",
    )(*far(x_own, x_oth))


def join_kernel(far_rows, _block, out):
    out[pl.ds(CUT3, ROWS >> 3), :] = far_rows[...]


def join(block, far_rows):
    return pl.pallas_call(
        join_kernel,
        out_shape=pltpu.VMEM(block.shape, block.dtype),
        in_specs=[HELD, HELD],
        out_specs=HELD,
        input_output_aliases={1: 0},
        compiler_params=params(3),
    )(*held(far_rows, block))


def collect_kernel(*refs):
    for n, ref in enumerate(refs[:-1]):
        refs[-1][pl.ds(n * (ROWS >> 3), ROWS >> 3), :] = ref[pl.ds(CUT2, ROWS >> 3), :]


def collect(blocks):
    return pl.pallas_call(
        collect_kernel,
        out_shape=pltpu.VMEM((len(blocks) * (ROWS >> 3), WB), blocks[0].dtype),
        in_specs=[HELD] * len(blocks),
        out_specs=HELD,
        compiler_params=params(3),
    )(*held(*blocks))


def payload_kernel(block, part, parts, w, out, sem):
    core = lax.rem(lax.axis_index("ctx"), 2)
    size = w.shape[0] // 2 // parts
    rows = pl.ds(pl.multiple_of((core * parts + part) * size, size), size)
    source = w.at[rows] if block is None else w.at[rows, pl.ds(pl.multiple_of(block() * WB, HD), WB)]
    copy = pltpu.make_async_copy(source, out, sem.at[0])
    copy.start()
    copy.wait()


def payload(block, w, part=0, parts=1):
    return pl.pallas_call(
        lambda *refs: payload_kernel(block, part, parts, *refs),
        out_shape=pltpu.VMEM((w.shape[0] // 2 // parts, w.shape[1] if block is None else WB), w.dtype),
        in_specs=[FAR],
        out_specs=HELD,
        scratch_shapes=[pltpu.SemaphoreType.DMA((1,))],
        compiler_params=params(6),
    )(*far(w))


def first_block():
    odd = (lax.axis_index("ctx") // 16) % 2
    return 2 - 2 * lax.rem(lax.axis_index("dp") + odd, 2)


CUT2, CUT3 = ROWS >> 2, (ROWS >> 2) + (ROWS >> 3)


def proj_kernel(counts, slot, phases, for_keys, meta, x_all, w_loc, *rest):
    ins, rest = list(rest[: sum(counts)]), rest[sum(counts) :]
    remotes = [[ins.pop(0) for _ in range(n)] for n in counts]
    acc_in = None
    if 0 not in phases:
        acc_in, rest = rest[0], rest[1:]
    outs, (wbuf, wsem) = rest[:-2], rest[-2:]
    if 1 in phases:
        acc, outs = outs[-1], outs[:-1]
    else:
        acc = outs[0]
    half = w_loc.shape[0] // 2
    core = meta[META_CORE]
    src = meta[slot]
    col = pl.multiple_of(meta[slot + 1] * WB, HD)
    base = [pl.multiple_of((core if p == 0 else 1 - core) * half, half) for p in range(2)]
    for i, p in enumerate(phases):

        @pl.when(src == 0)
        def _():
            pltpu.make_async_copy(w_loc.at[pl.ds(base[p], half), pl.ds(col, WB)], wbuf.at[i], wsem.at[i]).start()

        for r in range(len(remotes) // len(phases)):
            parts = remotes[r * len(phases) + i]

            @pl.when(src == r + 1)
            def _():
                size = half // len(parts)
                for n, part in enumerate(parts):
                    pltpu.make_async_copy(part, wbuf.at[i, pl.ds(n * size, size)], wsem.at[i]).start()

    for i, p in enumerate(phases):
        pltpu.make_async_copy(w_loc.at[pl.ds(0, half), pl.ds(0, WB)], wbuf.at[i], wsem.at[i]).wait()
        for g in range(2):
            span = pl.ds(g * TOK, TOK)
            got = jnp.dot(x_all[span, pl.ds(base[p], half)], wbuf[i], preferred_element_type=jnp.float32)
            for h in range(HH):
                piece = got[:, h * HD : (h + 1) * HD]
                if p == 1:
                    piece = (acc if acc_in is None else acc_in)[h, span] + piece
                acc[h, span] = piece
                if p == 1:
                    outs[0][span, pl.ds(h * HD, HD)] = piece.astype(jnp.bfloat16)
    if 1 not in phases:
        return
    for h in range(HH):
        cols = pl.ds(h * HD, HD)
        kept = [
            acc[h, pl.ds(meta[META_OFF + j * HH + h], ROWS >> j, stride=1 << j), :].astype(jnp.bfloat16)
            for j in range(1, LEVELS)
        ]
        outs[1][:, cols] = kept[0]
        outs[2][pl.ds(0, CUT2), cols] = kept[1]
        outs[2][pl.ds(CUT2, ROWS >> 3), cols] = kept[2]
        if for_keys:
            outs[2][pl.ds(CUT3, ROWS >> 3), cols] = kept[2]
            outs[3][:, cols] = kept[2]


def project(meta, slot, x_all, w_loc, remotes, for_keys=False, phases=(0, 1), acc=None):
    depth = w_loc.shape[0]
    groups = [pair[p] for pair in remotes for p in phases]
    flat = [part for group in groups for part in group]
    acc_shape = ((HH, ROWS, HD), jnp.float32)
    if phases == (0,):
        shapes = [acc_shape]
    else:
        shapes = [(ROWS, WB), (ROWS >> 1, WB)] + ([(ROWS >> 1, WB), (ROWS >> 3, WB)] if for_keys else [(CUT3, WB)])
        shapes = [(n, jnp.bfloat16) for n in shapes]
    scratch = [pltpu.VMEM(*acc_shape)] if 1 in phases else []
    scratch += [pltpu.VMEM((len(phases), depth // 2, WB), jnp.bfloat16), pltpu.SemaphoreType.DMA((len(phases),))]
    more = [] if acc is None else [acc]
    return pl.pallas_call(
        lambda *refs: proj_kernel([len(g) for g in groups], slot, phases, for_keys, *refs),
        out_shape=[pltpu.VMEM(*n) for n in shapes],
        in_specs=[SCALARS, HELD, FAR] + [HELD] * (len(flat) + len(more)),
        out_specs=[HELD] * len(shapes),
        scratch_shapes=scratch,
        compiler_params=params(16),
        cost_estimate=pl.CostEstimate(
            flops=ROWS * depth * WB * len(phases), transcendentals=0, bytes_accessed=2 * (ROWS * depth + depth * WB + 2 * ROWS * WB)
        ),
    )(meta, *held(x_all), *far(w_loc), *held(*flat, *more))


def softmax_rows(q, keys, values, factor):
    scores = [lax.dot_general(q, k, (((1,), (1,)), ((), ())), preferred_element_type=jnp.float32) for k in keys]
    top = scores[0].max(axis=1, keepdims=True)
    for s in scores[1:]:
        top = jnp.maximum(top, s.max(axis=1, keepdims=True))
    total, blend = 0.0, 0.0
    for s, v in zip(scores, values):
        e = jnp.exp2((s - top) * factor)
        total = total + e.sum(axis=1, keepdims=True)
        blend = blend + jnp.dot(e.astype(jnp.bfloat16), v, preferred_element_type=jnp.float32)
    return blend, top * factor, total


def lanes(column):
    return jnp.broadcast_to(column, (column.shape[0], HD))


def merge(state, where, blend, top, total):
    acc_ref, top_ref, total_ref = state
    old = top_ref[where]
    top = lanes(top)
    newest = jnp.maximum(old, top)
    former, fresh = jnp.exp2(old - newest), jnp.exp2(top - newest)
    acc_ref[where] = acc_ref[where] * former + blend * fresh
    total_ref[where] = total_ref[where] * former + lanes(total) * fresh
    top_ref[where] = newest


def choose(meta, firsts, seconds):
    f_is_k = jnp.full((1, 1), meta[META_FK], jnp.int32) == 1
    f = firsts[0] if len(firsts) == 1 else jnp.concatenate(firsts, axis=0)
    s = seconds[0] if len(seconds) == 1 else jnp.concatenate(seconds, axis=0)
    return [jnp.where(f_is_k, f, s)], [jnp.where(f_is_k, s, f)]


def level0_kernel(factor, meta, q_ref, f_ref, s_ref, acc_ref, top_ref, total_ref):
    for h in range(HH):
        cols = pl.ds(h * HD, HD)
        keys, values = choose(meta, [f_ref[:, cols]], [s_ref[:, cols]])
        for start in range(0, ROWS, TOK):
            blend, top, total = softmax_rows(q_ref[pl.ds(start, TOK), cols], keys, values, factor)
            acc_ref[h, pl.ds(start, TOK), :] = blend
            top_ref[h, pl.ds(start, TOK), :] = lanes(top)
            total_ref[h, pl.ds(start, TOK), :] = lanes(total)


def level1_kernel(factor, meta, q_ref, f0, f1, s0, s1, *refs):
    for h in range(HH):
        cols = pl.ds(h * HD, HD)
        keys, values = choose(meta, [f0[:, cols], f1[:, cols]], [s0[:, cols], s1[:, cols]])
        where = (h, pl.ds(meta[META_OFF + HH + h], TOK, stride=2), slice(None))
        merge(refs[3:], where, *softmax_rows(q_ref[:, cols], keys, values, factor))


def level23_kernel(factor, meta, q_ref, *refs):
    fs, f_far, ss, (own_ref, oth_ref, *state) = refs[:4], refs[4], refs[5:9], refs[12:]
    third = ROWS >> 3
    for h in range(HH):
        cols = pl.ds(h * HD, HD)
        for level, low, rows in ((2, 0, CUT2), (3, CUT2, third)):
            if level == 2:
                firsts, seconds = [f[:CUT2, cols] for f in fs], [s[:CUT2, cols] for s in ss]
            else:
                firsts = [r for n, f in enumerate(fs) for r in (f[CUT2:, cols], f_far[pl.ds(n * third, third), cols])]
                seconds = [s[CUT2:, cols] for s in ss]
            keys, values = choose(meta, firsts, seconds)
            where = (h, pl.ds(meta[META_OFF + level * HH + h], rows, stride=1 << level), slice(None))
            merge(state, where, *softmax_rows(q_ref[pl.ds(low, rows), cols], keys, values, factor))
        share = state[0][h] * (1.0 / state[2][h])
        own_ref[:, cols] = share[:TOK].astype(jnp.bfloat16)
        oth_ref[:, cols] = share[TOK:].astype(jnp.bfloat16)


STATE = [((HH, ROWS, HD), jnp.float32)] * 3


def attend(kernel, meta, arrays, outs, rows, alias=None):
    factor = HD ** (-0.5) * LOG2E
    return pl.pallas_call(
        lambda *refs: kernel(factor, *refs),
        out_shape=[pltpu.VMEM(*o) for o in outs],
        in_specs=[SCALARS] + [HELD] * len(arrays),
        out_specs=[HELD] * len(outs),
        input_output_aliases=alias or {},
        compiler_params=params(20),
        cost_estimate=pl.CostEstimate(
            flops=4 * rows * ROWS * WB, transcendentals=rows * ROWS * HH, bytes_accessed=2 * (rows + 2 * ROWS) * WB
        ),
    )(meta, *held(*arrays))


def tile_of(t, core_rows, w_loc, rem):
    cols = pl.ds((t % 2) * WB, WB)
    return w_loc[core_rows, cols] if t < 2 else rem[:, cols]


def out_own_kernel(meta, att, w_loc, rem, part):
    rows = pl.ds(pl.multiple_of(meta[META_CORE] * WB, HD), WB)
    for t in range(4):
        part[t] = jnp.dot(att[...], tile_of(t, rows, w_loc, rem), preferred_element_type=jnp.float32)


def out_oth_kernel(meta, att, w_loc, rem, part, out, buf, sem):
    rows = pl.ds(pl.multiple_of((1 - meta[META_CORE]) * WB, HD), WB)
    d = meta[META_DP]
    copies = []
    for t in range(4):
        got = part[t] + jnp.dot(att[...], tile_of(t, rows, w_loc, rem), preferred_element_type=jnp.float32)
        buf[t] = got.astype(jnp.bfloat16)
        col = (d if t < 2 else 1 - d) * (2 * WB) + (t % 2) * WB
        copies.append(pltpu.make_async_copy(buf.at[t], out.at[:, pl.ds(pl.multiple_of(col, HD), WB)], sem.at[t]))
        copies[-1].start()
    for copy in copies:
        copy.wait()


def out_project(kernel, meta, arrays, out_shape, out_spec, scratch):
    return pl.pallas_call(
        kernel,
        out_shape=out_shape,
        in_specs=[SCALARS] + [HELD] * len(arrays),
        out_specs=out_spec,
        scratch_shapes=scratch,
        compiler_params=params(16),
        cost_estimate=pl.CostEstimate(flops=8 * TOK * WB * WB, transcendentals=0, bytes_accessed=8 * WB * WB + 8 * TOK * WB),
    )(meta, *held(*arrays))


def local(tokens, qkv_weight, out_weight, offsets):
    depth = qkv_weight.shape[0]
    meta = pl.pallas_call(
        scalars_kernel,
        out_shape=jax.ShapeDtypeStruct((META_OFF + LEVELS * HH,), jnp.int32),
        in_specs=[SCALARS],
        out_specs=SCALARS,
        compiler_params=params(1),
        name="scalars",
    )(offsets)

    x_own = tokens.reshape(TOK, depth)
    parts = range(2)
    first_own = [send(payload(first_block, qkv_weight, n, 2), to_y) for n in parts]
    x_oth = send(x_own, to_core)
    side_own = [send(payload(lambda: 1, qkv_weight), to_y)]
    x_all = stage(x_own, x_oth)
    first_fwd = [send(first_own[n], to_core) for n in parts]
    relay_own = [send(first_own[n], to_x) for n in parts]
    relay_fwd = [send(relay_own[n], to_core) for n in parts]
    side_fwd = [send(side_own[0], to_core)]

    def along_z(rows):
        pair = send(rows, to_z1)
        ring = send(rows, to_z3)
        return [rows, pair, ring, send(pair, to_z3)]

    first = project(meta, META_FSRC, x_all, qkv_weight, [(first_own, first_fwd)])
    f23 = along_z(first[2])
    f1_pair = send(first[1], to_z1)
    f3_far = send(collect(f23), to_y2)

    everything = [(first_own, first_fwd), (relay_own, relay_fwd), (side_own, side_fwd)]
    (acc,) = project(meta, META_SSRC, x_all, qkv_weight, everything, phases=(0,))
    second = project(meta, META_SSRC, x_all, qkv_weight, everything, True, phases=(1,), acc=acc)
    s_far = send(second[3], to_y2)
    s23 = along_z(join(second[2], s_far))
    s1_pair = send(second[1], to_z1)
    queries = project(meta, META_QSRC, x_all, qkv_weight, everything)

    rem_own = send(payload(None, out_weight), to_y)
    rem_oth = send(rem_own, to_core)

    state = attend(level0_kernel, meta, [queries[0], first[0], second[0]], STATE, ROWS)
    arrays = [queries[1], first[1], f1_pair, second[1], s1_pair, *state]
    state = attend(level1_kernel, meta, arrays, STATE, ROWS >> 1, {6: 0, 7: 1, 8: 2})
    arrays = [queries[2], *f23, f3_far, *s23, *state]
    outs = [((TOK, WB), jnp.bfloat16)] * 2 + STATE
    att, att_send, *_ = attend(level23_kernel, meta, arrays, outs, CUT3, {11: 2, 12: 3, 13: 4})
    att_oth = send(att_send, to_core)
    part = out_project(
        out_own_kernel, meta, [att, out_weight, rem_own], pltpu.VMEM((4, TOK, WB), jnp.float32), HELD, []
    )
    mixed = out_project(
        out_oth_kernel,
        meta,
        [att_oth, out_weight, rem_oth, part],
        jax.ShapeDtypeStruct((TOK, 4 * WB), jnp.bfloat16),
        FAR,
        [pltpu.VMEM((4, TOK, WB), jnp.bfloat16), pltpu.SemaphoreType.DMA((4,))],
    )
    return mixed.reshape(1, TOK, mixed.shape[1])


def solution(mesh):
    in_specs = (P("dp", "ctx", None), P(None, "dp"), P(None, "dp"), P())
    out_specs = P("dp", "ctx", None)

    return jax.shard_map(local, mesh=mesh, in_specs=in_specs, out_specs=out_specs, check_vma=False)
```

```python
import jax
import jax.numpy as jnp
from jax import lax
from jax.experimental import pallas as pl
from jax.experimental.pallas import tpu as pltpu
from jax.sharding import PartitionSpec as P


TOK = 384
ROWS = 2 * TOK
HD = 128
HH = 5
WB = HH * HD
LEVELS = 4
LOG2E = 1.4426950408889634

META_CORE, META_FSRC, META_FBLK, META_SSRC, META_SBLK, META_QSRC, META_QBLK, META_FK, META_DP = range(9)
META_OFF = 16


def lin(x, y, z, c):
    return (y % 2) * 64 + (((x % 4) * 2 + (y % 4) // 2) * 4 + z % 4) * 2 + c


def send(block, target):
    route = []
    for x in range(4):
        for y in range(4):
            for z in range(4):
                for c in range(2):
                    goal = target(x, y, z, c)
                    if goal is not None:
                        route.append((lin(x, y, z, c), lin(*goal)))
    return lax.ppermute(block, ("dp", "ctx"), route)


def to_core(x, y, z, c):
    return (x, y, z, 1 - c)


def to_y(x, y, z, c):
    return (x, y - 1 if c == 0 else y + 1, z, c)


def to_x(x, y, z, c):
    return (x - 1 if c == 0 else x + 1, y, z, c)


def to_z1(x, y, z, c):
    return (x, y, z ^ 1, c)


def to_z3(x, y, z, c):
    return (x, y, z ^ 3, c)


def to_y2(x, y, z, c):
    return (x, y + 2, z, c)


def held(*arrays):
    return [pltpu.with_memory_space_constraint(a, pltpu.VMEM) for a in arrays]


def far(*arrays):
    return [pltpu.with_memory_space_constraint(a, pltpu.HBM) for a in arrays]


HELD = pl.BlockSpec(memory_space=pltpu.VMEM)
SCALARS = pl.BlockSpec(memory_space=pltpu.SMEM)
FAR = pl.BlockSpec(memory_space=pltpu.HBM)


def params(mib):
    return pltpu.CompilerParams(vmem_limit_bytes=mib << 20)


def scalars_kernel(offsets, meta):
    d = lax.axis_index("dp")
    ctx = lax.axis_index("ctx")
    core = lax.rem(ctx, 2)
    odd = lax.rem(ctx // 16, 2)
    place = 2 * d + core

    def pick(*by_place):
        got = jnp.int32(by_place[3])
        for n in range(3):
            got = jnp.where(place == n, by_place[n], got)
        return got

    meta[META_CORE] = core
    meta[META_DP] = d
    meta[META_FSRC], meta[META_FBLK] = pick(0, 1, 0, 0), pick(2, 0, 1, 0)
    meta[META_SSRC], meta[META_SBLK] = pick(3, 2, 1 + odd, 0), pick(0, 0, 0, 2)
    meta[META_QSRC], meta[META_QBLK] = pick(0, 0, 2 - odd, 3), pick(0, 1, 0, 0)
    meta[META_FK] = pick(1, 1 - odd, 0, 1)
    for n in range(9, META_OFF):
        meta[n] = 0
    for j in range(LEVELS):
        for h in range(HH):
            meta[META_OFF + j * HH + h] = jnp.where(core == 0, offsets[j, h], offsets[j, HH + h])


def stage_kernel(x_own, x_oth, x_all, sem):
    copies = [pltpu.make_async_copy(x, x_all.at[pl.ds(g * TOK, TOK)], sem.at[g]) for g, x in enumerate((x_own, x_oth))]
    for copy in copies:
        copy.start()
    for copy in copies:
        copy.wait()


def stage(x_own, x_oth):
    return pl.pallas_call(
        stage_kernel,
        out_shape=pltpu.VMEM((ROWS, x_own.shape[1]), x_own.dtype),
        in_specs=[FAR, FAR],
        out_specs=HELD,
        scratch_shapes=[pltpu.SemaphoreType.DMA((2,))],
        compiler_params=params(6),
        name="stage",
    )(*far(x_own, x_oth))


def join_kernel(far_rows, _block, out):
    out[pl.ds(CUT3, ROWS >> 3), :] = far_rows[...]


def join(block, far_rows):
    return pl.pallas_call(
        join_kernel,
        out_shape=pltpu.VMEM(block.shape, block.dtype),
        in_specs=[HELD, HELD],
        out_specs=HELD,
        input_output_aliases={1: 0},
        compiler_params=params(3),
    )(*held(far_rows, block))


def collect_kernel(*refs):
    for n, ref in enumerate(refs[:-1]):
        refs[-1][pl.ds(n * (ROWS >> 3), ROWS >> 3), :] = ref[pl.ds(CUT2, ROWS >> 3), :]


def collect(blocks):
    return pl.pallas_call(
        collect_kernel,
        out_shape=pltpu.VMEM((len(blocks) * (ROWS >> 3), WB), blocks[0].dtype),
        in_specs=[HELD] * len(blocks),
        out_specs=HELD,
        compiler_params=params(3),
    )(*held(*blocks))


def payload_kernel(block, part, parts, w, out, sem):
    core = lax.rem(lax.axis_index("ctx"), 2)
    size = w.shape[0] // 2 // parts
    rows = pl.ds(pl.multiple_of((core * parts + part) * size, size), size)
    source = w.at[rows] if block is None else w.at[rows, pl.ds(pl.multiple_of(block() * WB, HD), WB)]
    copy = pltpu.make_async_copy(source, out, sem.at[0])
    copy.start()
    copy.wait()


def payload(block, w, part=0, parts=1):
    return pl.pallas_call(
        lambda *refs: payload_kernel(block, part, parts, *refs),
        out_shape=pltpu.VMEM((w.shape[0] // 2 // parts, w.shape[1] if block is None else WB), w.dtype),
        in_specs=[FAR],
        out_specs=HELD,
        scratch_shapes=[pltpu.SemaphoreType.DMA((1,))],
        compiler_params=params(6),
    )(*far(w))


def first_block():
    odd = (lax.axis_index("ctx") // 16) % 2
    return 2 - 2 * lax.rem(lax.axis_index("dp") + odd, 2)


CUT2, CUT3 = ROWS >> 2, (ROWS >> 2) + (ROWS >> 3)


def proj_kernel(counts, slot, phases, for_keys, meta, x_all, w_loc, *rest):
    ins, rest = list(rest[: sum(counts)]), rest[sum(counts) :]
    remotes = [[ins.pop(0) for _ in range(n)] for n in counts]
    acc_in = None
    if 0 not in phases:
        acc_in, rest = rest[0], rest[1:]
    outs, (wbuf, wsem) = rest[:-2], rest[-2:]
    if 1 in phases:
        acc, outs = outs[-1], outs[:-1]
    else:
        acc = outs[0]
    half = w_loc.shape[0] // 2
    core = meta[META_CORE]
    src = meta[slot]
    col = pl.multiple_of(meta[slot + 1] * WB, HD)
    base = [pl.multiple_of((core if p == 0 else 1 - core) * half, half) for p in range(2)]
    for i, p in enumerate(phases):

        @pl.when(src == 0)
        def _():
            pltpu.make_async_copy(w_loc.at[pl.ds(base[p], half), pl.ds(col, WB)], wbuf.at[i], wsem.at[i]).start()

        for r in range(len(remotes) // len(phases)):
            parts = remotes[r * len(phases) + i]

            @pl.when(src == r + 1)
            def _():
                size = half // len(parts)
                for n, part in enumerate(parts):
                    pltpu.make_async_copy(part, wbuf.at[i, pl.ds(n * size, size)], wsem.at[i]).start()

    for i, p in enumerate(phases):
        pltpu.make_async_copy(w_loc.at[pl.ds(0, half), pl.ds(0, WB)], wbuf.at[i], wsem.at[i]).wait()
        for g in range(2):
            span = pl.ds(g * TOK, TOK)
            got = jnp.dot(x_all[span, pl.ds(base[p], half)], wbuf[i], preferred_element_type=jnp.float32)
            for h in range(HH):
                piece = got[:, h * HD : (h + 1) * HD]
                if p == 1:
                    piece = (acc if acc_in is None else acc_in)[h, span] + piece
                acc[h, span] = piece
                if p == 1:
                    outs[0][span, pl.ds(h * HD, HD)] = piece.astype(jnp.bfloat16)
    if 1 not in phases:
        return
    for h in range(HH):
        cols = pl.ds(h * HD, HD)
        kept = [
            acc[h, pl.ds(meta[META_OFF + j * HH + h], ROWS >> j, stride=1 << j), :].astype(jnp.bfloat16)
            for j in range(1, LEVELS)
        ]
        outs[1][:, cols] = kept[0]
        outs[2][pl.ds(0, CUT2), cols] = kept[1]
        outs[2][pl.ds(CUT2, ROWS >> 3), cols] = kept[2]
        if for_keys:
            outs[2][pl.ds(CUT3, ROWS >> 3), cols] = kept[2]
            outs[3][:, cols] = kept[2]


def project(meta, slot, x_all, w_loc, remotes, for_keys=False, phases=(0, 1), acc=None):
    depth = w_loc.shape[0]
    groups = [pair[p] for pair in remotes for p in phases]
    flat = [part for group in groups for part in group]
    acc_shape = ((HH, ROWS, HD), jnp.float32)
    if phases == (0,):
        shapes = [acc_shape]
    else:
        shapes = [(ROWS, WB), (ROWS >> 1, WB)] + ([(ROWS >> 1, WB), (ROWS >> 3, WB)] if for_keys else [(CUT3, WB)])
        shapes = [(n, jnp.bfloat16) for n in shapes]
    scratch = [pltpu.VMEM(*acc_shape)] if 1 in phases else []
    scratch += [pltpu.VMEM((len(phases), depth // 2, WB), jnp.bfloat16), pltpu.SemaphoreType.DMA((len(phases),))]
    more = [] if acc is None else [acc]
    return pl.pallas_call(
        lambda *refs: proj_kernel([len(g) for g in groups], slot, phases, for_keys, *refs),
        out_shape=[pltpu.VMEM(*n) for n in shapes],
        in_specs=[SCALARS, HELD, FAR] + [HELD] * (len(flat) + len(more)),
        out_specs=[HELD] * len(shapes),
        scratch_shapes=scratch,
        compiler_params=params(16),
        cost_estimate=pl.CostEstimate(
            flops=ROWS * depth * WB * len(phases), transcendentals=0, bytes_accessed=2 * (ROWS * depth + depth * WB + 2 * ROWS * WB)
        ),
    )(meta, *held(x_all), *far(w_loc), *held(*flat, *more))


def softmax_rows(q, keys, values, factor):
    scores = [lax.dot_general(q, k, (((1,), (1,)), ((), ())), preferred_element_type=jnp.float32) for k in keys]
    top = scores[0].max(axis=1, keepdims=True)
    for s in scores[1:]:
        top = jnp.maximum(top, s.max(axis=1, keepdims=True))
    total, blend = 0.0, 0.0
    for s, v in zip(scores, values):
        e = jnp.exp2((s - top) * factor)
        total = total + e.sum(axis=1, keepdims=True)
        blend = blend + jnp.dot(e.astype(jnp.bfloat16), v, preferred_element_type=jnp.float32)
    return blend, top * factor, total


def lanes(column):
    return jnp.broadcast_to(column, (column.shape[0], HD))


def merge(state, where, blend, top, total):
    acc_ref, top_ref, total_ref = state
    old = top_ref[where]
    top = lanes(top)
    newest = jnp.maximum(old, top)
    former, fresh = jnp.exp2(old - newest), jnp.exp2(top - newest)
    acc_ref[where] = acc_ref[where] * former + blend * fresh
    total_ref[where] = total_ref[where] * former + lanes(total) * fresh
    top_ref[where] = newest


def choose(meta, firsts, seconds):
    f_is_k = jnp.full((1, 1), meta[META_FK], jnp.int32) == 1
    f = firsts[0] if len(firsts) == 1 else jnp.concatenate(firsts, axis=0)
    s = seconds[0] if len(seconds) == 1 else jnp.concatenate(seconds, axis=0)
    return [jnp.where(f_is_k, f, s)], [jnp.where(f_is_k, s, f)]


def level0_kernel(factor, meta, q_ref, f_ref, s_ref, acc_ref, top_ref, total_ref):
    for h in range(HH):
        cols = pl.ds(h * HD, HD)
        keys, values = choose(meta, [f_ref[:, cols]], [s_ref[:, cols]])
        for start in range(0, ROWS, TOK):
            blend, top, total = softmax_rows(q_ref[pl.ds(start, TOK), cols], keys, values, factor)
            acc_ref[h, pl.ds(start, TOK), :] = blend
            top_ref[h, pl.ds(start, TOK), :] = lanes(top)
            total_ref[h, pl.ds(start, TOK), :] = lanes(total)


def level1_kernel(factor, meta, q_ref, f0, f1, s0, s1, *refs):
    for h in range(HH):
        cols = pl.ds(h * HD, HD)
        keys, values = choose(meta, [f0[:, cols], f1[:, cols]], [s0[:, cols], s1[:, cols]])
        where = (h, pl.ds(meta[META_OFF + HH + h], TOK, stride=2), slice(None))
        merge(refs[3:], where, *softmax_rows(q_ref[:, cols], keys, values, factor))


def level23_kernel(factor, meta, q_ref, *refs):
    fs, f_far, ss, (own_ref, oth_ref, *state) = refs[:4], refs[4], refs[5:9], refs[12:]
    third = ROWS >> 3
    for h in range(HH):
        cols = pl.ds(h * HD, HD)
        for level, low, rows in ((2, 0, CUT2), (3, CUT2, third)):
            if level == 2:
                firsts, seconds = [f[:CUT2, cols] for f in fs], [s[:CUT2, cols] for s in ss]
            else:
                firsts = [r for n, f in enumerate(fs) for r in (f[CUT2:, cols], f_far[pl.ds(n * third, third), cols])]
                seconds = [s[CUT2:, cols] for s in ss]
            keys, values = choose(meta, firsts, seconds)
            where = (h, pl.ds(meta[META_OFF + level * HH + h], rows, stride=1 << level), slice(None))
            merge(state, where, *softmax_rows(q_ref[pl.ds(low, rows), cols], keys, values, factor))
        share = state[0][h] * (1.0 / state[2][h])
        own_ref[:, cols] = share[:TOK].astype(jnp.bfloat16)
        oth_ref[:, cols] = share[TOK:].astype(jnp.bfloat16)


STATE = [((HH, ROWS, HD), jnp.float32)] * 3


def attend(kernel, meta, arrays, outs, rows, alias=None):
    factor = HD ** (-0.5) * LOG2E
    return pl.pallas_call(
        lambda *refs: kernel(factor, *refs),
        out_shape=[pltpu.VMEM(*o) for o in outs],
        in_specs=[SCALARS] + [HELD] * len(arrays),
        out_specs=[HELD] * len(outs),
        input_output_aliases=alias or {},
        compiler_params=params(20),
        cost_estimate=pl.CostEstimate(
            flops=4 * rows * ROWS * WB, transcendentals=rows * ROWS * HH, bytes_accessed=2 * (rows + 2 * ROWS) * WB
        ),
    )(meta, *held(*arrays))


TILES = tuple((side, low, wide) for side in range(2) for low, wide in ((0, 768), (768, 512)))


def tile_of(tile, core_rows, w_loc, rem):
    side, low, wide = tile
    return w_loc[core_rows, pl.ds(low, wide)] if side == 0 else rem[:, pl.ds(low, wide)]


def out_own_kernel(meta, att, w_loc, rem, part):
    rows = pl.ds(pl.multiple_of(meta[META_CORE] * WB, HD), WB)
    for tile in TILES:
        cols = pl.ds(tile[0] * 2 * WB + tile[1], tile[2])
        part[:, cols] = jnp.dot(att[...], tile_of(tile, rows, w_loc, rem), preferred_element_type=jnp.float32)


def out_oth_kernel(meta, att, w_loc, rem, part, out, buf, sem):
    rows = pl.ds(pl.multiple_of((1 - meta[META_CORE]) * WB, HD), WB)
    d = meta[META_DP]
    copies = []
    for n, tile in enumerate(TILES):
        side, low, wide = tile
        cols = pl.ds(side * 2 * WB + low, wide)
        got = part[:, cols] + jnp.dot(att[...], tile_of(tile, rows, w_loc, rem), preferred_element_type=jnp.float32)
        buf[:, cols] = got.astype(jnp.bfloat16)
        to = (d if side == 0 else 1 - d) * (2 * WB) + low
        copies.append(pltpu.make_async_copy(buf.at[:, cols], out.at[:, pl.ds(pl.multiple_of(to, HD), wide)], sem.at[n]))
        copies[-1].start()
    for copy in copies:
        copy.wait()


def out_project(kernel, meta, arrays, out_shape, out_spec, scratch):
    return pl.pallas_call(
        kernel,
        out_shape=out_shape,
        in_specs=[SCALARS] + [HELD] * len(arrays),
        out_specs=out_spec,
        scratch_shapes=scratch,
        compiler_params=params(16),
        cost_estimate=pl.CostEstimate(flops=8 * TOK * WB * WB, transcendentals=0, bytes_accessed=8 * WB * WB + 8 * TOK * WB),
    )(meta, *held(*arrays))


def local(tokens, qkv_weight, out_weight, offsets):
    depth = qkv_weight.shape[0]
    meta = pl.pallas_call(
        scalars_kernel,
        out_shape=jax.ShapeDtypeStruct((META_OFF + LEVELS * HH,), jnp.int32),
        in_specs=[SCALARS],
        out_specs=SCALARS,
        compiler_params=params(1),
        name="scalars",
    )(offsets)

    x_own = tokens.reshape(TOK, depth)
    parts = range(2)
    first_own = [send(payload(first_block, qkv_weight, n, 2), to_y) for n in parts]
    x_oth = send(x_own, to_core)
    side_own = [send(payload(lambda: 1, qkv_weight), to_y)]
    x_all = stage(x_own, x_oth)
    first_fwd = [send(first_own[n], to_core) for n in parts]
    relay_own = [send(first_own[n], to_x) for n in parts]
    relay_fwd = [send(relay_own[n], to_core) for n in parts]
    side_fwd = [send(side_own[0], to_core)]

    def along_z(rows):
        pair = send(rows, to_z1)
        ring = send(rows, to_z3)
        return [rows, pair, ring, send(pair, to_z3)]

    first = project(meta, META_FSRC, x_all, qkv_weight, [(first_own, first_fwd)])
    f23 = along_z(first[2])
    f1_pair = send(first[1], to_z1)
    f3_far = send(collect(f23), to_y2)

    everything = [(first_own, first_fwd), (relay_own, relay_fwd), (side_own, side_fwd)]
    (acc,) = project(meta, META_SSRC, x_all, qkv_weight, everything, phases=(0,))
    second = project(meta, META_SSRC, x_all, qkv_weight, everything, True, phases=(1,), acc=acc)
    s_far = send(second[3], to_y2)
    s23 = along_z(join(second[2], s_far))
    s1_pair = send(second[1], to_z1)
    queries = project(meta, META_QSRC, x_all, qkv_weight, everything)

    rem_own = send(payload(None, out_weight), to_y)
    rem_oth = send(rem_own, to_core)

    state = attend(level0_kernel, meta, [queries[0], first[0], second[0]], STATE, ROWS)
    arrays = [queries[1], first[1], f1_pair, second[1], s1_pair, *state]
    state = attend(level1_kernel, meta, arrays, STATE, ROWS >> 1, {6: 0, 7: 1, 8: 2})
    arrays = [queries[2], *f23, f3_far, *s23, *state]
    outs = [((TOK, WB), jnp.bfloat16)] * 2 + STATE
    att, att_send, *_ = attend(level23_kernel, meta, arrays, outs, CUT3, {11: 2, 12: 3, 13: 4})
    att_oth = send(att_send, to_core)
    part = out_project(
        out_own_kernel, meta, [att, out_weight, rem_own], pltpu.VMEM((TOK, 4 * WB), jnp.float32), HELD, []
    )
    mixed = out_project(
        out_oth_kernel,
        meta,
        [att_oth, out_weight, rem_oth, part],
        jax.ShapeDtypeStruct((TOK, 4 * WB), jnp.bfloat16),
        FAR,
        [pltpu.VMEM((TOK, 4 * WB), jnp.bfloat16), pltpu.SemaphoreType.DMA((len(TILES),))],
    )
    return mixed.reshape(1, TOK, mixed.shape[1])


def solution(mesh):
    in_specs = (P("dp", "ctx", None), P(None, "dp"), P(None, "dp"), P())
    out_specs = P("dp", "ctx", None)

    return jax.shard_map(local, mesh=mesh, in_specs=in_specs, out_specs=out_specs, check_vma=False)
```
